32 devices in a mesh: grp: 4 (over y, core), fsdp: 8 (over z, x).
Axes of the slice: x: 2, y: 2, z: 4, core: 2. Of those that a mesh axis runs over, the one named last changes fastest.
Arguments:
- traj_hidden: bfloat16 [32768, 4096], P(('grp', 'fsdp')), may hold values from -6 to 6
- traj_tokens: int32 [32768], P(('grp', 'fsdp')), may hold values from 0 to 511
- traj_action: int32 [32768], P(('grp', 'fsdp')), may hold values from 0 to 511
- traj_return: float32 [32768], P(('grp', 'fsdp')), may hold values from -6 to 6
- traj_episode: int32 [32, 1024], P(('grp', 'fsdp')), may hold values from 0 to 7, never falling along the last dimension, each value on 1 to 512 neighbouring positions
- roll_hidden: bfloat16 [2048, 4096], P(('grp', 'fsdp')), may hold values from -6 to 6
- roll_tokens: int32 [2048], P(('grp', 'fsdp')), may hold values from 0 to 511
- roll_action: int32 [2048], P(('grp', 'fsdp')), may hold values from 0 to 511
- station_table: bfloat16 [512, 4096], replicated, may hold values from -3 to 3
- norm_gain: float32 [4096], replicated, may hold values from 0.7 to 3.9
- head_weight: bfloat16 [4096, 512], P('fsdp'), may hold values from -6 to 6
Outputs:
- new_head: bfloat16 [4096, 512], P('fsdp')
- action_logp: float32 [2048], P(('grp', 'fsdp'))
- episode_logp: float32 [32], P(('grp', 'fsdp'))
The draws below stay inside these ranges and needn't reach their ends.
Inputs may be any that keep to these rules, and one draw needn't show every extreme that they name: `traj_episode`: within each block of 1024 tokens the episode numbers never fall and every number 0 to 7 occurs.
All inputs are finite; a program needn't handle non-finite values.
Results may differ from the reference program's by a relative error of at most 0.0034.
Values may be sent and summed in bfloat16 or wider, within the bound.
No kernel may reach another device: no remote copies, remote signals or barrier semaphores. Data moves between devices by JAX's collectives and lax.ppermute only.
A program may use at most 64 MiB of HBM per device.

```python
import math
import jax
import jax.numpy as jnp
import numpy as np
from jax import lax

D = 4096
ACTIONS = 512
STATIONS = 512
TOKL = 1024
EPI_BLK = 8
STEPS = 64
NBLK = 32
LROWS = 32768
RROWS = 2048


def draw_norm_gain(key, part):
    place = jnp.arange(D, dtype=jnp.float32) / D
    spread = jax.random.uniform(key, (D,), jnp.float32, 0.7, 1.3)
    return spread * jnp.sqrt(1.0 + 2.0 * place)


def draw_head_weight(key, part):
    base = jax.random.normal(jax.random.fold_in(key, 11), (D, ACTIONS), jnp.float32) / math.sqrt(D)
    return jnp.clip(base, -6.0, 6.0).astype(jnp.bfloat16)


def plant(values, key, least, top_value):
    spot = [jax.random.randint(jax.random.fold_in(key, axis), (), 0, length) for axis, length in enumerate(values.shape)]
    widest = values.shape.index(max(values.shape))
    beside = spot[:widest] + [(spot[widest] + 1) % values.shape[widest]] + spot[widest + 1:]
    return values.at[tuple(spot)].set(least).at[tuple(beside)].set(top_value)


def raised(entries, own_key, source, target, parts, factor):
    owner, partner = [(jnp.arange(entries.shape[position]) // (entries.shape[position] // parts)).reshape([-1 if axis == position else 1 for axis in range(entries.ndim)]) for position in (source, target)]
    chosen = jax.random.permutation(own_key, parts)[partner]
    strong = (owner == chosen) | (owner == (partner + parts // 2) % parts)
    return jnp.where(strong, factor * entries, entries)


def shard_levels(rng, extent, shards, low, high):
    def one(axis_at, parts):
        heights = jax.random.uniform(jax.random.fold_in(jax.random.fold_in(rng, 6), axis_at), (parts,), jnp.float32, low / len(shards), high / len(shards))
        return jnp.repeat(jnp.exp(heights), extent[axis_at] // parts).reshape((-1,) + (1,) * (len(extent) - axis_at - 1))

    level = one(*shards[0])
    for cut in shards[1:]:
        level = level * one(*cut)
    return level


def rank_bounds(number_of, skew):
    portions = [(1 << 20) // math.isqrt(grade ** skew) + 1 for grade in range(1, number_of + 1)]
    scale = 1 + sum(portions) // (1 << 30)
    return np.cumsum(np.array([max(1, weight // scale) for weight in portions]))


def skewed_ids(own_key, extent, number_of, skew):
    grid = rank_bounds(number_of, skew)
    ticket = jax.random.randint(jax.random.fold_in(own_key, 1), extent, 0, int(grid[number_of - 1]))
    grade = jnp.searchsorted(jnp.asarray(grid, jnp.int32), ticket, side="right")
    return jax.random.permutation(jax.random.fold_in(own_key, 2), number_of)[grade].astype(jnp.int32)


def length_profile(amount, total, bound, slope):
    loads = [(1 << 20) // math.isqrt(grade ** slope) + 1 for grade in range(2, amount + 1)]
    surplus, given = total - bound - (amount - 1), [1] * (amount - 1)
    while surplus > 0:
        candidates = [i for i in range(amount - 1) if given[i] < bound]
        pool, remaining = sum([loads[i] for i in candidates]), surplus
        for i in candidates:
            addition = min(bound - given[i], max(1, remaining * loads[i] // pool), surplus)
            given[i] = given[i] + addition
            surplus = surplus - addition
    return np.array([bound] + given)


def ragged_sizes(stream_key, amount, total, most, lean):
    if amount == 2:
        one = jax.random.randint(stream_key, (), max(1, total - most), min(most, total - 1) + 1)
        return jnp.stack([one, total - one])
    lengths = jnp.asarray(length_profile(amount, total, most, lean), jnp.int32)
    twos = (amount - 1) // 2
    giver, receiver = lengths[1:1 + 2 * twos:2], lengths[2:2 + 2 * twos:2]
    margin = jnp.minimum(giver - 1, most - receiver)
    shifted = jax.random.randint(jax.random.fold_in(stream_key, 1), (twos,), 0, 1 << 20) % (margin + 1)
    lengths = lengths.at[1:1 + 2 * twos:2].set(giver - shifted).at[2:2 + 2 * twos:2].set(receiver + shifted)
    return lengths[jax.random.permutation(jax.random.fold_in(stream_key, 2), amount)]


def scatter_about(key, extent, scale, bound, pieces=(), kind=jnp.bfloat16):
    array = scale * jax.random.normal(key, extent, jnp.float32)
    if pieces:
        array = array * shard_levels(key, extent, pieces, -0.22, 0.18)
    return jnp.clip(array, -bound, bound).astype(kind)


def gaussian_with(own_key, dims, width, most, cuts, heavy, kind=jnp.bfloat16):
    entries = width * jax.random.normal(own_key, dims, jnp.float32)
    if cuts:
        entries = entries * shard_levels(own_key, dims, cuts, -0.22, 0.18)
    return jnp.clip(raised(entries, jax.random.fold_in(own_key, 3), *heavy), -most, most).astype(kind)


def setup_inputs(seed: int = 0) -> dict:
    key_list = jax.random.split(jax.random.key(seed), 12)
    traj_hidden = gaussian_with(key_list[0], (LROWS, D), 1.0, 6.0, ((0, 32),), (0, 1, 32, 2.75))
    traj_tokens = plant(skewed_ids(key_list[1], (LROWS,), STATIONS, 2), jax.random.fold_in(key_list[1], 3), 0, STATIONS - 1).astype(jnp.int32)
    traj_action = plant(jax.random.randint(key_list[2], (LROWS,), 0, ACTIONS), jax.random.fold_in(key_list[2], 1), 0, ACTIONS - 1).astype(jnp.int32)
    traj_return = scatter_about(key_list[3], (LROWS,), 1.0, 6.0, ((0, 32),), jnp.float32)
    traj_episode = jax.vmap(lambda own: jnp.searchsorted(jnp.cumsum(ragged_sizes(own, EPI_BLK, TOKL, TOKL // 2, 1)), jnp.arange(TOKL), side="right"))(jax.random.split(key_list[4], NBLK)).reshape((NBLK, TOKL)).astype(jnp.int32)
    roll_hidden = scatter_about(key_list[5], (RROWS, D), 1.0, 6.0, ((0, 32),))
    roll_tokens = plant(skewed_ids(key_list[6], (RROWS,), STATIONS, 2), jax.random.fold_in(key_list[6], 3), 0, STATIONS - 1).astype(jnp.int32)
    roll_action = plant(jax.random.randint(key_list[7], (RROWS,), 0, ACTIONS), jax.random.fold_in(key_list[7], 1), 0, ACTIONS - 1).astype(jnp.int32)
    station_table = scatter_about(key_list[8], (STATIONS, D), 0.5, 3.0)
    norm_gain = draw_norm_gain(jax.random.fold_in(key_list[11], 71), 0)
    head_weight = draw_head_weight(jax.random.fold_in(key_list[11], 71), 0)
    return {"traj_hidden": traj_hidden, "traj_tokens": traj_tokens, "traj_action": traj_action, "traj_return": traj_return, "traj_episode": traj_episode, "roll_hidden": roll_hidden, "roll_tokens": roll_tokens, "roll_action": roll_action, "station_table": station_table, "norm_gain": norm_gain, "head_weight": head_weight}


step_length = 8.0

def station_rows(hidden, tokens, table, gain):
    mixed = hidden.astype(jnp.float32) + table[tokens].astype(jnp.float32)
    power = lax.optimization_barrier(jnp.mean(mixed * mixed, axis=-1, keepdims=True))
    return (mixed * lax.rsqrt(power + 1e-05) * gain).astype(jnp.bfloat16)

def product(left, right):
    return jnp.dot(left.astype(jnp.float32), right.astype(jnp.float32), precision=lax.Precision.HIGHEST)

def picked_logp(logits, actions):
    top = lax.optimization_barrier(jnp.max(logits, axis=-1, keepdims=True))
    total = jnp.log(lax.optimization_barrier(jnp.sum(jnp.exp(logits - top), axis=-1))) + top[:, 0]
    chosen = (actions[:, None] == jnp.arange(ACTIONS, dtype=jnp.int32)[None, :]).astype(jnp.float32)
    return lax.optimization_barrier(jnp.sum(logits * chosen, axis=-1)) - total

def reference(traj_hidden, traj_tokens, traj_action, traj_return, traj_episode, roll_hidden, roll_tokens, roll_action, station_table, norm_gain, head_weight):
    features = station_rows(traj_hidden, traj_tokens, station_table, norm_gain)
    logits = product(features, head_weight)
    top = lax.optimization_barrier(jnp.max(logits, axis=-1, keepdims=True))
    expo = jnp.exp(logits - top)
    probs = expo / lax.optimization_barrier(jnp.sum(expo, axis=-1, keepdims=True))
    member = (traj_episode[:, :, None] == jnp.arange(EPI_BLK, dtype=jnp.int32)[None, None, :]).astype(jnp.float32)
    returns = traj_return.reshape(traj_episode.shape)
    sums = jnp.einsum('bte,bt->be', member, returns, precision=lax.Precision.HIGHEST)
    counts = lax.optimization_barrier(jnp.sum(member, axis=1))
    baseline = jnp.einsum('bte,be->bt', member, sums / counts, precision=lax.Precision.HIGHEST).reshape(-1)
    advantage = traj_return - baseline
    chosen = (traj_action[:, None] == jnp.arange(ACTIONS, dtype=jnp.int32)[None, :]).astype(jnp.float32)
    scores = (advantage[:, None] * (probs - chosen)).astype(jnp.bfloat16)
    grad = jnp.dot(features.astype(jnp.float32).T, scores.astype(jnp.float32), precision=lax.Precision.HIGHEST)
    gnorm = jnp.sqrt(jnp.sum(grad * grad) + 1e-06)
    new_head = (head_weight.astype(jnp.float32) - step_length * grad / gnorm).astype(jnp.bfloat16)
    rollout = station_rows(roll_hidden, roll_tokens, station_table, norm_gain)
    roll_logits = product(rollout, new_head)
    action_logp = picked_logp(roll_logits, roll_action)
    episode_logp = lax.optimization_barrier(jnp.sum(action_logp.reshape(-1, STEPS), axis=1))
    return (new_head, action_logp, episode_logp)
```

```python
import functools

import jax
import jax.numpy as jnp
from jax import lax
from jax.experimental import pallas as pl
from jax.experimental.pallas import tpu as pltpu
from jax.sharding import PartitionSpec as P


EPI_BLK = 8
STEPS = 64
AXES = ("grp", "fsdp")
F32, BF16, I32 = jnp.float32, jnp.bfloat16, jnp.int32

step_length = 8.0


def column(row):
    blocks = [jnp.broadcast_to(row[:, at : at + 128], (128, 128)) for at in range(0, row.shape[1], 128)]
    return jnp.concatenate([jnp.transpose(b) for b in blocks], axis=0)


def features_kernel(
    chunks, tab_ref, hidden_ref, roll_ref, token_ref, table_ref, gain_ref, return_ref, episode_ref, action_ref,
    feats_ref, turned_ref, roll_out_ref, roll_rel_ref, advantage_ref, chosen_ref,
    lookup_ref, mixed_ref, power_ref,
):
    step = pl.program_id(0)
    rows, wide = hidden_ref.shape
    few = roll_ref.shape[0]
    half = wide // 2

    @pl.when(step == 0)
    def _():
        down = column(token_ref[...])[: rows + few]
        lane = lax.broadcasted_iota(I32, down.shape, 1)
        for at in range(0, table_ref.shape[0], 128):
            lookup_ref[:, at : at + 128] = jnp.where(down == lane + at, 1.0, 0.0).astype(BF16)
        power_ref[...] = jnp.zeros_like(power_ref)
        returns, episode = return_ref[...], episode_ref[...]
        baseline = jnp.zeros_like(returns)
        for e in range(EPI_BLK):
            member = episode == e
            total = jnp.sum(jnp.where(member, returns, 0.0), axis=-1, keepdims=True)
            count = jnp.sum(jnp.where(member, 1.0, 0.0), axis=-1, keepdims=True)
            baseline = jnp.where(member, total / jnp.maximum(count, 1.0), baseline)
        advantage_ref[...] = column(returns - baseline)
        chosen_ref[...] = column(action_ref[...])

    @pl.when(step < chunks)
    def _():
        embedded = jnp.dot(lookup_ref[...], table_ref[...], preferred_element_type=F32)
        for lo, n, ref in ((0, rows, hidden_ref), (rows, few, roll_ref)):
            mixed = ref[...].astype(F32) + embedded[lo : lo + n]
            mixed_ref[step, lo : lo + n] = mixed
            square = mixed * mixed
            power = square[:, :128]
            for at in range(128, wide, 128):
                power = power + square[:, at : at + 128]
            power_ref[lo : lo + n] += power

    @pl.when(step == chunks - 1)
    def _():
        mean = jnp.sum(power_ref[...], axis=-1, keepdims=True) / (chunks * wide)
        power_ref[...] = jnp.broadcast_to(lax.rsqrt(mean + 1e-05), power_ref.shape)

    @pl.when(step >= chunks)
    def _():
        scale = jnp.concatenate([power_ref[...]] * (wide // 128), axis=1)
        value = (mixed_ref[step - chunks] * scale * gain_ref[...]).astype(BF16)
        feats_ref[0], feats_ref[1] = value[:rows, :half], value[:rows, half:]
        roll_out_ref[0], roll_out_ref[1] = value[rows:, :half], value[rows:, half:]
        roll_rel_ref[0] = value[rows:]
        turned_ref[...] = jnp.transpose(value[:rows]).reshape(turned_ref.shape)


def features_call(shard, tab, hidden, roll, tokens, table, gain, returns, episode, action):
    rows, width = hidden.shape
    half, few, chunks = shard // 2, roll.shape[0], width // shard
    quarter = half // 2
    full = lambda shape: pl.BlockSpec(shape, lambda i, t: (0,) * len(shape))
    before = lambda i: jnp.minimum(i, chunks - 1)
    after = lambda i: jnp.maximum(i - chunks, 0)
    return pl.pallas_call(
        functools.partial(features_kernel, chunks),
        grid_spec=pltpu.PrefetchScalarGridSpec(
            num_scalar_prefetch=1,
            grid=(2 * chunks,),
            in_specs=[
                pl.BlockSpec((rows, shard), lambda i, t: (0, before(i))),
                pl.BlockSpec((few, shard), lambda i, t: (0, before(i))),
                full(tokens.shape),
                pl.BlockSpec((table.shape[0], shard), lambda i, t: (0, before(i))),
                pl.BlockSpec((1, shard), lambda i, t: (0, after(i))),
                full((1, rows)),
                full((1, rows)),
                full((1, rows)),
            ],
            out_specs=[
                pl.BlockSpec((2, rows, half), lambda i, t: (after(i), 0, 0)),
                pl.BlockSpec((4, quarter, rows), lambda i, t: (after(i), 0, 0)),
                pl.BlockSpec((2, few, half), lambda i, t: (after(i), 0, 0)),
                pl.BlockSpec((1, few, shard), lambda i, t: (t[0] ^ after(i), 0, 0)),
                full((rows, 128)),
                full((rows, 128)),
            ],
            scratch_shapes=[
                pltpu.VMEM((rows + few, table.shape[0]), BF16),
                pltpu.VMEM((chunks, rows + few, shard), F32),
                pltpu.VMEM((rows + few, 128), F32),
            ],
        ),
        out_shape=[
            jax.ShapeDtypeStruct((2 * chunks, rows, half), BF16),
            jax.ShapeDtypeStruct((4 * chunks, quarter, rows), BF16),
            jax.ShapeDtypeStruct((2 * chunks, few, half), BF16),
            jax.ShapeDtypeStruct((chunks, few, shard), BF16),
            jax.ShapeDtypeStruct((rows, 128), F32),
            jax.ShapeDtypeStruct((rows, 128), I32),
        ],
        cost_estimate=pl.CostEstimate(
            flops=4 * rows * width * table.shape[0], transcendentals=0, bytes_accessed=8 * rows * width
        ),
        name="features",
    )(tab, hidden, roll, tokens, table, gain, returns, episode, action)


def logits_kernel(pieces, has_acc, last, tab_ref, *refs):
    count = sum(pieces)
    feats, refs = refs[:count], refs[count:]
    heads, refs = refs[: len(pieces)], refs[len(pieces) :]
    left = jnp.concatenate([ref[0] for ref in feats], axis=1)
    right = jnp.concatenate([ref[p] for ref, n in zip(heads, pieces) for p in range(n)], axis=0)
    logits = jnp.dot(left, right, preferred_element_type=F32)
    if has_acc:
        logits = logits + refs[0][...]
        refs = refs[1:]
    if not last:
        refs[0][...] = logits
        return
    advantage_ref, chosen_ref, out_ref = refs
    actions = logits.shape[1]
    top = jnp.max(logits, axis=1, keepdims=True)
    expo = jnp.exp(logits - top)
    probs = expo / jnp.sum(expo, axis=1, keepdims=True)
    advantage, action = advantage_ref[...], chosen_ref[...]
    lane = lax.broadcasted_iota(I32, action.shape, 1)
    for at in range(0, actions, 128):
        chosen = jnp.where(action == lane + at, 1.0, 0.0)
        out_ref[:, at : at + 128] = (advantage * (probs[:, at : at + 128] - chosen)).astype(BF16)


def logits_call(feats, tab, at, heads, acc=None, last=None):
    _, rows, half = feats.shape
    actions = heads[0].shape[2]
    pieces = tuple(h.shape[0] for h in heads)
    count = sum(pieces)
    tall = 512
    block = pl.BlockSpec((tall, actions), lambda i, t: (i, 0))
    thin = pl.BlockSpec((tall, 128), lambda i, t: (i, 0))
    in_specs = [
        pl.BlockSpec((1, tall, half), functools.partial(lambda k, i, t: (t[k], i, 0), at + k)) for k in range(count)
    ]
    in_specs += [pl.BlockSpec(h.shape, lambda i, t: (0, 0, 0)) for h in heads]
    args = [feats] * count + list(heads)
    if acc is not None:
        in_specs.append(block)
        args.append(acc)
    if last is not None:
        in_specs += [thin, thin]
        args += list(last)
    return pl.pallas_call(
        functools.partial(logits_kernel, pieces, acc is not None, last is not None),
        grid_spec=pltpu.PrefetchScalarGridSpec(
            num_scalar_prefetch=1, grid=(rows // tall,), in_specs=in_specs, out_specs=block
        ),
        out_shape=jax.ShapeDtypeStruct((rows, actions), F32 if last is None else BF16),
        cost_estimate=pl.CostEstimate(
            flops=2 * rows * count * half * actions, transcendentals=0, bytes_accessed=2 * rows * count * half
        ),
        name="logits",
    )(tab, *args)


def grad_kernel(count, tab_ref, scores_ref, *refs):
    feats, out_ref = refs[:count], refs[count]
    left = jnp.concatenate([ref[0] for ref in feats], axis=0)
    out = jnp.dot(left, scores_ref[...], preferred_element_type=F32)
    out_ref[...] = out.astype(out_ref.dtype).reshape(out_ref.shape)


def grad_call(scores, turned, tab, at, count, dtype):
    _, quarter, rows = turned.shape
    actions = scores.shape[1]
    each = min(count, 4)
    return pl.pallas_call(
        functools.partial(grad_kernel, each),
        grid_spec=pltpu.PrefetchScalarGridSpec(
            num_scalar_prefetch=1,
            grid=(count // each,),
            in_specs=[pl.BlockSpec((rows, actions), lambda i, t: (0, 0))]
            + [
                pl.BlockSpec((1, quarter, rows), functools.partial(lambda k, i, t: (t[at + i * each + k], 0, 0), k))
                for k in range(each)
            ],
            out_specs=pl.BlockSpec((each, quarter, actions), lambda i, t: (i, 0, 0)),
        ),
        out_shape=jax.ShapeDtypeStruct((count, quarter, actions), dtype),
        cost_estimate=pl.CostEstimate(
            flops=2 * rows * count * quarter * actions, transcendentals=0, bytes_accessed=2 * rows * count * quarter
        ),
        name="grad",
    )(tab, scores, *[turned] * each)


def old_logits_kernel(pieces, tab_ref, roll_ref, *refs):
    heads, out_ref = refs[:-1], refs[-1]
    blocks = [ref[p] for ref, n in zip(heads, pieces) for p in range(n)]
    left = jnp.concatenate([roll_ref[tab_ref[k]] for k in range(len(blocks))], axis=1)
    out_ref[...] = jnp.dot(left, jnp.concatenate(blocks, axis=0), preferred_element_type=F32)


def old_logits_call(roll, tab, heads):
    pieces = tuple(h.shape[0] for h in heads)
    full = lambda shape: pl.BlockSpec(shape, lambda i, t: (0,) * len(shape))
    out = (roll.shape[1], heads[0].shape[2])
    return pl.pallas_call(
        functools.partial(old_logits_kernel, pieces),
        grid_spec=pltpu.PrefetchScalarGridSpec(
            num_scalar_prefetch=1,
            grid=(1,),
            in_specs=[full(roll.shape)] + [full(h.shape) for h in heads],
            out_specs=full(out),
        ),
        out_shape=jax.ShapeDtypeStruct(out, F32),
        name="old_logits",
    )(tab, roll, *heads)


def share_kernel(count, tab_ref, own_ref, other_ref, *refs):
    rolls, grad_ref, outs = refs[:count], refs[count], refs[count + 1 :]
    quarter, actions = own_ref.shape[1:]
    for k in range(2):
        grad_ref[tab_ref[k]] = own_ref[k]
        grad_ref[tab_ref[2 + k]] = other_ref[k]
    grad = grad_ref[...].reshape(4 * quarter, actions)
    wide = grad.astype(F32)
    square = jnp.sum(wide * wide, keepdims=True)
    first = square.astype(BF16).astype(F32)
    second = (square - first).astype(BF16).astype(F32)
    third = square - first - second
    rows = rolls[0].shape[1]
    left = jnp.concatenate([ref[0] for ref in rolls], axis=0)
    part = jnp.dot(left, grad, preferred_element_type=F32)
    line = lax.broadcasted_iota(I32, (16, actions), 0)
    foot = jnp.where(line == 0, first, jnp.where(line == 1, second, third)).astype(BF16)
    for m in range(count):
        outs[m][:rows] = part[m * rows : (m + 1) * rows].astype(BF16)
        outs[m][rows:] = foot


def share_call(tab, own, other, rolls):
    quarter, actions = own.shape[1:]
    rows = rolls[0].shape[1]
    full = lambda shape: pl.BlockSpec(shape, lambda i, t: (0,) * len(shape))
    shape = (rows + 16, actions)
    return pl.pallas_call(
        functools.partial(share_kernel, len(rolls)),
        grid_spec=pltpu.PrefetchScalarGridSpec(
            num_scalar_prefetch=1,
            grid=(1,),
            in_specs=[full(own.shape)] * 2 + [full(rolls[0].shape)] * len(rolls),
            out_specs=[full((4, quarter, actions))] + [full(shape)] * len(rolls),
        ),
        out_shape=[jax.ShapeDtypeStruct((4, quarter, actions), BF16)]
        + [jax.ShapeDtypeStruct(shape, BF16)] * len(rolls),
        name="share",
    )(tab, own, other, *rolls)


def finish_kernel(count, old_ref, chosen_ref, head_ref, grad_ref, *refs):
    parts, (head_out, logp_out, episode_out) = refs[:count], refs[count:]
    rows, actions = old_ref.shape
    update = jnp.zeros((rows, actions), F32)
    square = jnp.zeros((1, actions), F32)
    for ref in parts:
        update += ref[:rows].astype(F32)
        foot = ref[rows:].astype(F32)
        square += foot[0:1] + foot[1:2] + foot[2:3]
    gnorm = jnp.sqrt(square + 1e-06)
    logits = old_ref[...] - step_length * update / gnorm
    top = jnp.max(logits, axis=-1, keepdims=True)
    total = jnp.log(jnp.sum(jnp.exp(logits - top), axis=-1, keepdims=True)) + top
    logp = jnp.sum(logits * chosen_ref[...], axis=-1, keepdims=True) - total
    here = lax.broadcasted_iota(I32, (rows, rows), 0) == lax.broadcasted_iota(I32, (rows, rows), 1)
    logp_out[...] = jnp.sum(jnp.where(here, logp, 0.0), axis=0, keepdims=True)
    episodes = rows // STEPS
    mine = lax.broadcasted_iota(I32, (rows, episodes), 0) // STEPS == lax.broadcasted_iota(I32, (rows, episodes), 1)
    episode_out[...] = jnp.sum(jnp.where(mine, logp, 0.0), axis=0, keepdims=True)
    head_out[...] = (head_ref[...].astype(F32) - step_length * grad_ref[...].astype(F32) / gnorm).astype(BF16)


def finish_call(old, chosen, head, grad, parts):
    rows = old.shape[0]
    return pl.pallas_call(
        functools.partial(finish_kernel, len(parts)),
        out_shape=[
            jax.ShapeDtypeStruct(head.shape, BF16),
            jax.ShapeDtypeStruct((1, rows), F32),
            jax.ShapeDtypeStruct((1, rows // STEPS), F32),
        ],
        name="finish",
    )(old, chosen, head, grad, *parts)


X, NEAR, FAR, CORE, Y = 1, 2, 4, 8, 16
GATHER = ((FAR, NEAR, X), (FAR, X, NEAR))
REDUCE = ((FAR, NEAR, Y, X), (FAR, X, NEAR, Y))


def span(basis):
    return [
        functools.reduce(lambda a, b: a ^ b, [m for k, m in enumerate(basis) if address >> k & 1], 0)
        for address in range(1 << len(basis))
    ]


def swap(value, mask):
    masks = mask if isinstance(mask, tuple) else (mask, mask)
    shards, devices = lax.axis_size("fsdp"), lax.axis_size(AXES)
    return lax.ppermute(value, AXES, [(i, i ^ masks[i // shards & 1]) for i in range(devices)])


def local_cube(
    traj_hidden, traj_tokens, traj_action, traj_return, traj_episode,
    roll_hidden, roll_tokens, roll_action, station_table, norm_gain, head_weight,
):
    shard, actions = head_weight.shape
    half, few = shard // 2, roll_hidden.shape[0]
    place = lax.axis_index("fsdp")
    group = lax.axis_index("grp")
    core, level = group % 2, group // 2

    def addresses(masks, flip):
        spans = [jnp.array(span(m), I32) for m in masks]
        mine = jnp.where(core == flip, spans[0], spans[1])
        return place ^ (mine & 7), level ^ (mine >> 4)

    halves = [2 * addresses(GATHER, flip)[0] + (core if flip == 0 else 1 - core) for flip in (0, 1)]
    order = jnp.concatenate([halves[0][:4], halves[1][:4], halves[0][4:], halves[1][4:]]).astype(I32)
    quarters = []
    for flip in (0, 1):
        at, up = addresses(REDUCE, flip)
        quarters.append(4 * at + 2 * (core if flip == 0 else 1 - core) + up)
    blocks = jnp.concatenate([quarters[1][8:], quarters[0][8:], quarters[1][:8], quarters[0][:8]]).astype(I32)
    lines = jnp.stack([2 * core + level, 2 * core + 1 - level, 2 - 2 * core + level, 3 - 2 * core - level])
    lines = lines.astype(I32)

    held = lax.dynamic_slice_in_dim(head_weight, core * half, half, 0)[None]
    came = swap(held, tuple(g[0] for g in GATHER))
    held = jnp.concatenate([held, came], axis=0)
    came = swap(held, tuple(g[1] for g in GATHER))
    held = jnp.concatenate([held, came], axis=0)
    came = swap(held, tuple(g[2] for g in GATHER))
    other_held = swap(held, CORE)
    other_came = swap(came, CORE)

    tokens = jnp.concatenate([traj_tokens, jnp.pad(roll_tokens, (0, 128 - few))]).reshape(1, -1)
    features, turned, roll_blocks, roll_parts, advantage, chosen = features_call(
        shard, place[None].astype(I32), traj_hidden, roll_hidden, tokens, station_table,
        norm_gain.reshape(1, -1), traj_return.reshape(1, -1), traj_episode, traj_action.reshape(1, -1),
    )
    logits = logits_call(features, order, 0, [held, other_held])
    logits = logits_call(features, order, 8, [came], acc=logits)
    scores = logits_call(features, order, 12, [other_came], acc=logits, last=(advantage, chosen))

    terms = []
    for part in range(2):
        out = grad_call(scores, turned, blocks, 16 * part, 8, BF16)
        crossed = swap(out, CORE)
        keep = grad_call(scores, turned, blocks, 16 * part + 8, 8, F32)
        terms.append([keep, crossed])
    (high, low), n = terms[::-1][1], 8
    send = (high + low.astype(F32)).astype(BF16)
    came_back = swap(send, tuple(r[3] for r in REDUCE))
    parts = terms[1] + [came_back]
    for k in (2, 1, 0):
        n = 1 << k
        send = sum(t[n : 2 * n].astype(F32) for t in parts).astype(BF16)
        parts = [t[:n] for t in parts] + [swap(send, tuple(r[k] for r in REDUCE))]
    own = sum(t.astype(F32) for t in parts).astype(BF16)
    own = jnp.concatenate([own, swap(own, Y)], axis=0)
    other = swap(own, CORE)

    rolls = [roll_parts[0:1]]
    for m in range(1, 8):
        rolls.append(swap(roll_parts[m : m + 1], m))
    grad, *shares = share_call(lines, own, other, rolls)
    for m in range(1, 8):
        shares[m] = swap(shares[m], m)
    old = old_logits_call(roll_blocks, order, [held, other_held, came, other_came])
    picked = (roll_action[:, None] == jnp.arange(actions, dtype=I32)[None, :]).astype(F32)
    new_head, action_logp, episode_logp = finish_call(old, picked, head_weight, grad.reshape(shard, actions), shares)
    return new_head, action_logp.reshape(-1), episode_logp.reshape(-1)


def station_rows(hidden, tokens, table, gain):
    stations = table.shape[0]
    lookup = (tokens[:, None] == jnp.arange(stations, dtype=I32)[None, :]).astype(BF16)
    embedded = jnp.dot(lookup, table, preferred_element_type=F32)
    mixed = hidden.astype(F32) + embedded
    power = jnp.mean(mixed * mixed, axis=-1, keepdims=True)
    return (mixed * lax.rsqrt(power + 1e-05) * gain).astype(BF16)


def picked_logp(logits, actions):
    top = jnp.max(logits, axis=-1, keepdims=True)
    total = jnp.log(jnp.sum(jnp.exp(logits - top), axis=-1)) + top[:, 0]
    chosen = (actions[:, None] == jnp.arange(logits.shape[1], dtype=I32)[None, :]).astype(F32)
    return jnp.sum(logits * chosen, axis=-1) - total


def episode_advantage(returns, episode):
    member = (episode[:, None] == jnp.arange(EPI_BLK, dtype=I32)[None, :]).astype(F32)
    sums = jnp.dot(member.T, returns, precision=lax.Precision.HIGHEST)
    counts = jnp.sum(member, axis=0)
    baseline = jnp.dot(member, sums / counts, precision=lax.Precision.HIGHEST)
    return returns - baseline


def local_plain(
    traj_hidden, traj_tokens, traj_action, traj_return, traj_episode,
    roll_hidden, roll_tokens, roll_action, station_table, norm_gain, head_weight,
):
    shard, actions = head_weight.shape
    features = station_rows(traj_hidden, traj_tokens, station_table, norm_gain)
    rollout = station_rows(roll_hidden, roll_tokens, station_table, norm_gain)
    advantage = episode_advantage(traj_return, traj_episode[0])
    full_old = lax.all_gather(head_weight, "fsdp", axis=0, tiled=True)
    logits = jnp.dot(features, full_old, preferred_element_type=F32)
    top = jnp.max(logits, axis=-1, keepdims=True)
    expo = jnp.exp(logits - top)
    probs = expo / jnp.sum(expo, axis=-1, keepdims=True)
    chosen = (traj_action[:, None] == jnp.arange(actions, dtype=I32)[None, :]).astype(F32)
    scores = (advantage[:, None] * (probs - chosen)).astype(BF16)
    local_grad = lax.dot_general(features, scores, (((0,), (0,)), ((), ())), preferred_element_type=F32)
    grad = lax.psum(local_grad, AXES)
    gnorm = jnp.sqrt(jnp.sum(grad * grad) + 1e-06)
    new_full = (full_old.astype(F32) - step_length * grad / gnorm).astype(BF16)
    new_head = lax.dynamic_slice_in_dim(new_full, lax.axis_index("fsdp") * shard, shard, 0)
    roll_logits = jnp.dot(rollout, new_full, preferred_element_type=F32)
    action_logp = picked_logp(roll_logits, roll_action)
    return new_head, action_logp, jnp.sum(action_logp.reshape(-1, STEPS), axis=1)


def fits(args, groups, shards):
    hidden, episode, roll, table, head = args[0], args[4], args[5], args[8], args[10]
    if (groups, shards) != (4, 8) or episode.shape[0] != 1:
        return False
    aligned = head.shape[0] % 512 == 0 and head.shape[1] % 128 == 0 and table.shape[0] % 128 == 0
    whole = hidden.shape[1] == shards * head.shape[0] and hidden.shape[0] % 512 == 0
    return aligned and whole and roll.shape[0] <= 128 and roll.shape[0] % STEPS == 0


def solution(mesh):
    groups, shards = mesh.shape["grp"], mesh.shape["fsdp"]

    def local(*args):
        if not fits(args, groups, shards):
            return local_plain(*args)
        return local_cube(*args)

    both = P(AXES)
    wide = P(AXES, None)
    return jax.shard_map(
        local,
        mesh=mesh,
        in_specs=(wide, both, both, both, wide, wide, both, both, P(), P(), P("fsdp", None)),
        out_specs=(P("fsdp", None), both, both),
        check_vma=False,
    )
```

```python
import functools

import jax
import jax.numpy as jnp
import numpy as np
from jax import lax
from jax.experimental import pallas as pl
from jax.experimental.pallas import tpu as pltpu
from jax.sharding import PartitionSpec as P


EPI_BLK = 8
STEPS = 64
AXES = ("grp", "fsdp")
F32, BF16, I32 = jnp.float32, jnp.bfloat16, jnp.int32

step_length = 8.0


def room(mib):
    return pltpu.CompilerParams(vmem_limit_bytes=mib << 20)


def column(row):
    blocks = [jnp.broadcast_to(row[:, at : at + 128], (128, 128)) for at in range(0, row.shape[1], 128)]
    return jnp.concatenate([jnp.transpose(b) for b in blocks], axis=0)


SLOTS = 4


def features_kernel(start, last, tab_ref, hidden_ref, roll_ref, table_ref, *refs):
    small = [pltpu.make_async_copy(refs[k], refs[k - 7], refs[-1].at[k]) for k in range(6)]
    token_ref, roll_token_ref, gain_ref, return_ref, episode_ref, action_ref = refs[-7:-1]
    lookup_ref, mixed_ref, feats_stage, turned_stage, hidden_slots, roll_slots, table_slots, sems, out_sems = refs[-16:-7]
    outs = refs[6 + (2 if start else 0) : -16]
    feats_ref, turned_ref = outs[:2]
    rows, wide = hidden_slots.shape[1:]
    few, half, chunks = roll_slots.shape[1], wide // 2, mixed_ref.shape[0]
    groups = [(0, rows, hidden_slots)] + ([(rows, few, roll_slots)] if last else [])

    def fetch(chunk):
        slot, cut = chunk % SLOTS, slice(chunk * wide, (chunk + 1) * wide)
        moves = [(hidden_ref.at[start : start + rows, cut], hidden_slots), (table_ref.at[:, cut], table_slots)]
        if last:
            moves.append((roll_ref.at[:, cut], roll_slots))
        return [
            pltpu.make_async_copy(source, slots.at[slot], sems.at[k, slot]) for k, (source, slots) in enumerate(moves)
        ]

    def flush(chunk):
        slot = chunk % 2
        to = feats_ref.at[2 * chunk : 2 * chunk + 2, start : start + rows, :]
        turned_to = turned_ref.at[4 * chunk : 4 * chunk + 4, :, start : start + rows]
        return [
            pltpu.make_async_copy(feats_stage.at[slot], to, out_sems.at[0, slot]),
            pltpu.make_async_copy(turned_stage.at[slot], turned_to, out_sems.at[1, slot]),
        ]

    for copy in small:
        copy.start()
    for chunk in range(min(SLOTS, chunks)):
        for copy in fetch(chunk):
            copy.start()
    for copy in small:
        copy.wait()
    down = column(token_ref[:, start : start + rows])
    if last:
        here = lax.broadcasted_iota(I32, (few, few), 0) == lax.broadcasted_iota(I32, (few, few), 1)
        end = jnp.sum(jnp.where(here, roll_token_ref[...].astype(F32), 0.0), axis=1, keepdims=True).astype(I32)
        down = jnp.concatenate([down, jnp.broadcast_to(end, (few, 128))], axis=0)
    lane = lax.broadcasted_iota(I32, down.shape, 1)
    for at in range(0, table_ref.shape[0], 128):
        lookup_ref[:, at : at + 128] = jnp.where(down == lane + at, 1.0, 0.0).astype(BF16)
    powers = [jnp.zeros((n, 128), F32) for _, n, _ in groups]
    for chunk in range(chunks):
        slot = chunk % SLOTS
        for copy in fetch(chunk):
            copy.wait()
        embedded = jnp.dot(lookup_ref[...], table_slots[slot], preferred_element_type=F32)
        for g, (lo, n, ref) in enumerate(groups):
            mixed = ref[slot].astype(F32) + embedded[lo : lo + n]
            mixed_ref[chunk, lo : lo + n] = mixed
            square = mixed * mixed
            for at in range(0, wide, 128):
                powers[g] = powers[g] + square[:, at : at + 128]
        if chunk + SLOTS < chunks:
            for copy in fetch(chunk + SLOTS):
                copy.start()
    if last:
        returns, episode = return_ref[...], episode_ref[...]
        baseline = jnp.zeros_like(returns)
        for e in range(EPI_BLK):
            member = episode == e
            total = jnp.sum(jnp.where(member, returns, 0.0), axis=-1, keepdims=True)
            count = jnp.sum(jnp.where(member, 1.0, 0.0), axis=-1, keepdims=True)
            baseline = jnp.where(member, total / jnp.maximum(count, 1.0), baseline)
        outs[4][...] = column(returns - baseline)
        outs[5][...] = column(action_ref[...])
    scales = [lax.rsqrt(jnp.sum(p, axis=-1, keepdims=True) / (chunks * wide) + 1e-05) for p in powers]
    for chunk in range(chunks):
        slot, cut = chunk % 2, slice(chunk * wide, (chunk + 1) * wide)
        if chunk >= 2:
            for copy in flush(chunk - 2):
                copy.wait()
        value = (mixed_ref[chunk, :rows] * scales[0] * gain_ref[:, cut]).astype(BF16)
        feats_stage[slot, 0], feats_stage[slot, 1] = value[:, :half], value[:, half:]
        turned_stage[slot] = jnp.transpose(value).reshape(turned_stage.shape[1:])
        for copy in flush(chunk):
            copy.start()
        if last:
            value = (mixed_ref[chunk, rows:] * scales[1] * gain_ref[:, cut]).astype(BF16)
            roll_out_ref, roll_rel_ref = outs[2:4]
            roll_out_ref[2 * chunk], roll_out_ref[2 * chunk + 1] = value[:, :half], value[:, half:]
            roll_rel_ref[jnp.bitwise_xor(tab_ref[0], chunk)] = value
    for chunk in range(max(chunks - 2, 0), chunks):
        for copy in flush(chunk):
            copy.wait()


def features_call(shard, tab, start, rows, so_far, hidden, roll, table, tokens, roll_tokens, gain, returns, episode, action):
    tall, width = hidden.shape
    last = start + rows == tall
    half, few, chunks = shard // 2, roll.shape[0], width // shard
    quarter, all_rows = half // 2, rows + (few if last else 0)
    hbm, vmem = pl.BlockSpec(memory_space=pltpu.HBM), pl.BlockSpec(memory_space=pltpu.VMEM)
    anywhere = pl.BlockSpec(memory_space=pl.ANY)
    out_shape = [
        jax.ShapeDtypeStruct((2 * chunks, tall, half), BF16),
        jax.ShapeDtypeStruct((4 * chunks, quarter, tall), BF16),
        jax.ShapeDtypeStruct((2 * chunks, few, half), BF16),
        jax.ShapeDtypeStruct((chunks, few, shard), BF16),
        jax.ShapeDtypeStruct((tall, 128), F32),
        jax.ShapeDtypeStruct((tall, 128), I32),
    ]
    outs = 6 if last else 2
    args = (hidden, roll, table, tokens, roll_tokens, gain, returns, episode, action)
    args = [pltpu.with_memory_space_constraint(v, pltpu.HBM) for v in args]
    return pl.pallas_call(
        functools.partial(features_kernel, start, last),
        in_specs=[pl.BlockSpec(memory_space=pltpu.SMEM)] + [hbm] * 9 + [anywhere] * len(so_far),
        out_specs=([anywhere] * 2 + [vmem] * 4)[:outs],
        scratch_shapes=[
            pltpu.VMEM((all_rows, table.shape[0]), BF16),
            pltpu.VMEM((chunks, all_rows, shard), F32),
            pltpu.VMEM((2, 2, rows, half), BF16),
            pltpu.VMEM((2, 4, quarter, rows), BF16),
            pltpu.VMEM((SLOTS, rows, shard), BF16),
            pltpu.VMEM((SLOTS, few, shard), BF16),
            pltpu.VMEM((SLOTS, table.shape[0], shard), BF16),
            pltpu.SemaphoreType.DMA((3, SLOTS)),
            pltpu.SemaphoreType.DMA((2, 2)),
        ]
        + [pltpu.VMEM(v.shape, v.dtype) for v in args[3:]]
        + [pltpu.SemaphoreType.DMA((6,))],
        out_shape=out_shape[:outs],
        input_output_aliases={10 + k: k for k in range(len(so_far))},
        cost_estimate=pl.CostEstimate(
            flops=4 * rows * width * table.shape[0], transcendentals=0, bytes_accessed=8 * rows * width
        ),
        compiler_params=room(24),
        name="features",
    )(tab, *args, *so_far)


def join_heads(refs, pieces):
    halves = [
        jnp.concatenate([ref[p] for ref, n in zip(refs[c::2], pieces) for p in range(n)], axis=0) for c in range(2)
    ]
    return jnp.concatenate(halves, axis=1)


def logits_kernel(pieces, has_acc, last, tab_ref, *refs):
    count = sum(pieces)
    feats, refs = refs[:count], refs[count:]
    heads, refs = refs[: 2 * len(pieces)], refs[2 * len(pieces) :]
    left = jnp.concatenate([ref[0] for ref in feats], axis=1)
    right = join_heads(heads, pieces)
    logits = jnp.dot(left, right, preferred_element_type=F32)
    if has_acc:
        logits = logits + refs[0][...]
        refs = refs[1:]
    if not last:
        refs[0][...] = logits
        return
    advantage_ref, chosen_ref, out_ref = refs
    actions = logits.shape[1]
    top = jnp.max(logits, axis=1, keepdims=True)
    expo = jnp.exp(logits - top)
    probs = expo / jnp.sum(expo, axis=1, keepdims=True)
    advantage, action = advantage_ref[...], chosen_ref[...]
    lane = lax.broadcasted_iota(I32, action.shape, 1)
    for at in range(0, actions, 128):
        chosen = jnp.where(action == lane + at, 1.0, 0.0)
        out_ref[:, at : at + 128] = (advantage * (probs[:, at : at + 128] - chosen)).astype(BF16)


def logits_call(feats, tab, at, heads, acc=None, last=None):
    _, rows, half = feats.shape
    actions = 2 * heads[0][0].shape[2]
    pieces = tuple(h[0].shape[0] for h in heads)
    heads = [h for pair in heads for h in pair]
    count = sum(pieces)
    tall = 512
    block = pl.BlockSpec((tall, actions), lambda i, t: (i, 0))
    thin = pl.BlockSpec((tall, 128), lambda i, t: (i, 0))
    in_specs = [
        pl.BlockSpec((1, tall, half), functools.partial(lambda k, i, t: (t[k], i, 0), at + k)) for k in range(count)
    ]
    in_specs += [pl.BlockSpec(h.shape, lambda i, t: (0, 0, 0)) for h in heads]
    args = [feats] * count + list(heads)
    if acc is not None:
        in_specs.append(block)
        args.append(acc)
    if last is not None:
        in_specs += [thin, thin]
        args += list(last)
    return pl.pallas_call(
        functools.partial(logits_kernel, pieces, acc is not None, last is not None),
        grid_spec=pltpu.PrefetchScalarGridSpec(
            num_scalar_prefetch=1, grid=(rows // tall,), in_specs=in_specs, out_specs=block
        ),
        out_shape=jax.ShapeDtypeStruct((rows, actions), F32 if last is None else BF16),
        cost_estimate=pl.CostEstimate(
            flops=2 * rows * count * half * actions, transcendentals=0, bytes_accessed=2 * rows * count * half
        ),
        compiler_params=room(12),
        name="logits",
    )(tab, *args)


def grad_kernel(count, tab_ref, scores_ref, *refs):
    feats, extra, outs = refs[:count], refs[count:-2], refs[-2:]
    left = jnp.concatenate([ref[0] for ref in feats], axis=0)
    wide = outs[0].shape[2]
    for c, out_ref in enumerate(outs):
        right = scores_ref[:, c * wide : (c + 1) * wide]
        out = jnp.dot(left, right, preferred_element_type=F32).reshape(out_ref.shape)
        if extra:
            out = out + extra[c][...].astype(F32)
        out_ref[...] = out.astype(out_ref.dtype)


def grad_call(scores, turned, tab, at, count, dtype, *extra):
    _, quarter, rows = turned.shape
    actions = scores.shape[1]
    each = min(count, 4)
    block = pl.BlockSpec((each, quarter, actions // 2), lambda i, t: (i, 0, 0))
    return pl.pallas_call(
        functools.partial(grad_kernel, each),
        grid_spec=pltpu.PrefetchScalarGridSpec(
            num_scalar_prefetch=1,
            grid=(count // each,),
            in_specs=[pl.BlockSpec((rows, actions), lambda i, t: (0, 0))]
            + [
                pl.BlockSpec((1, quarter, rows), functools.partial(lambda k, i, t: (t[at + i * each + k], 0, 0), k))
                for k in range(each)
            ]
            + [block] * len(extra),
            out_specs=[block] * 2,
        ),
        out_shape=[jax.ShapeDtypeStruct((count, quarter, actions // 2), dtype)] * 2,
        cost_estimate=pl.CostEstimate(
            flops=2 * rows * count * quarter * actions, transcendentals=0, bytes_accessed=2 * rows * count * quarter
        ),
        compiler_params=room(10),
        name="grad",
    )(tab, scores, *[turned] * each, *extra)


def old_logits_kernel(pieces, tab_ref, roll_ref, *refs):
    heads, out_ref = refs[:-1], refs[-1]
    left = jnp.concatenate([roll_ref[tab_ref[ORDER + k]] for k in range(sum(pieces))], axis=1)
    out_ref[...] = jnp.dot(left, join_heads(heads, pieces), preferred_element_type=F32)


def old_logits_call(roll, tab, heads):
    pieces = tuple(h[0].shape[0] for h in heads)
    heads = [h for pair in heads for h in pair]
    full = lambda shape: pl.BlockSpec(shape, lambda i, t: (0,) * len(shape))
    out = (roll.shape[1], 2 * heads[0].shape[2])
    return pl.pallas_call(
        functools.partial(old_logits_kernel, pieces),
        grid_spec=pltpu.PrefetchScalarGridSpec(
            num_scalar_prefetch=1,
            grid=(1,),
            in_specs=[full(roll.shape)] + [full(h.shape) for h in heads],
            out_specs=full(out),
        ),
        out_shape=jax.ShapeDtypeStruct(out, F32),
        compiler_params=room(12),
        name="old_logits",
    )(tab, roll, *heads)


def split(value, wide):
    first = value.astype(BF16).astype(F32)
    second = (value - first).astype(BF16).astype(F32)
    line = lax.broadcasted_iota(I32, (16, wide), 0)
    third = jnp.where(line == 2, value - first - second, 0.0)
    return jnp.where(line == 0, first, jnp.where(line == 1, second, third)).astype(BF16)


def share_kernel(count, tab_ref, *refs):
    lines, rolls, grad_ref, outs = refs[:4], refs[4 : 4 + count], refs[4 + count], refs[5 + count :]
    quarter, actions = lines[0].shape[1:]
    for k, ref in enumerate(lines):
        grad_ref[tab_ref[LINES + k]] = ref[0]
    grad = grad_ref[...].reshape(4 * quarter, actions)
    wide = grad.astype(F32)
    square = jnp.sum(wide * wide, keepdims=True)
    rows = rolls[0].shape[1]
    left = jnp.concatenate([ref[0] for ref in rolls], axis=0)
    part = jnp.dot(left, grad, preferred_element_type=F32)
    foot = split(square, actions)
    far = count // 2
    for m in range(count):
        outs[m % far][m // far, :rows] = part[m * rows : (m + 1) * rows].astype(BF16)
        outs[m % far][m // far, rows:] = foot


def share_call(tab, lines, rolls):
    quarter, actions = lines[0].shape[1:]
    rows = rolls[0].shape[1]
    full = lambda shape: pl.BlockSpec(shape, lambda i, t: (0,) * len(shape))
    shape = (2, rows + 16, actions)
    return pl.pallas_call(
        functools.partial(share_kernel, len(rolls)),
        grid_spec=pltpu.PrefetchScalarGridSpec(
            num_scalar_prefetch=1,
            grid=(1,),
            in_specs=[full(lines[0].shape)] * 4 + [full(rolls[0].shape)] * len(rolls),
            out_specs=[full((4, quarter, actions))] + [full(shape)] * (len(rolls) // 2),
        ),
        out_shape=[jax.ShapeDtypeStruct((4, quarter, actions), BF16)]
        + [jax.ShapeDtypeStruct(shape, BF16)] * (len(rolls) // 2),
        compiler_params=room(6),
        name="share",
    )(tab, *lines, *rolls)


def join_kernel(*refs):
    parts, (stay_ref, send_ref) = refs[:-2], refs[-2:]
    rows = stay_ref.shape[0] - 16
    for k, out_ref in enumerate((stay_ref, send_ref)):
        total = parts[0][k].astype(F32)
        for ref in parts[1:]:
            total = total + ref[k].astype(F32)
        out_ref[:rows] = total[:rows].astype(out_ref.dtype)
        square = jnp.sum(total[rows:], axis=0, keepdims=True)
        if k == 0:
            out_ref[rows:] = jnp.broadcast_to(square, (16, square.shape[1]))
        else:
            out_ref[rows:] = split(square, square.shape[1])


def join_call(parts):
    shape = parts[0].shape[1:]
    return pl.pallas_call(
        join_kernel,
        out_shape=[jax.ShapeDtypeStruct(shape, F32), jax.ShapeDtypeStruct(shape, BF16)],
        compiler_params=room(4),
        name="join",
    )(*parts)


def finish_kernel(old_ref, chosen_ref, head_ref, grad_ref, stay_ref, far_ref, head_out, logp_out, episode_out):
    rows, _ = old_ref.shape
    update = stay_ref[:rows] + far_ref[:rows].astype(F32)
    square = stay_ref[rows : rows + 1] + jnp.sum(far_ref[rows:].astype(F32), axis=0, keepdims=True)
    gnorm = jnp.sqrt(square + 1e-06)
    logits = old_ref[...] - step_length * update / gnorm
    top = jnp.max(logits, axis=-1, keepdims=True)
    total = jnp.log(jnp.sum(jnp.exp(logits - top), axis=-1, keepdims=True)) + top
    logp = jnp.sum(logits * chosen_ref[...], axis=-1, keepdims=True) - total
    here = lax.broadcasted_iota(I32, (rows, rows), 0) == lax.broadcasted_iota(I32, (rows, rows), 1)
    logp_out[...] = jnp.sum(jnp.where(here, logp, 0.0), axis=0, keepdims=True)
    episodes = rows // STEPS
    mine = lax.broadcasted_iota(I32, (rows, episodes), 0) // STEPS == lax.broadcasted_iota(I32, (rows, episodes), 1)
    episode_out[...] = jnp.sum(jnp.where(mine, logp, 0.0), axis=0, keepdims=True)
    head_out[...] = (head_ref[...].astype(F32) - step_length * grad_ref[...].astype(F32) / gnorm).astype(BF16)


def finish_call(old, chosen, head, grad, stay, far):
    rows = old.shape[0]
    return pl.pallas_call(
        finish_kernel,
        out_shape=[
            jax.ShapeDtypeStruct(head.shape, BF16),
            jax.ShapeDtypeStruct((1, rows), F32),
            jax.ShapeDtypeStruct((1, rows // STEPS), F32),
        ],
        compiler_params=room(6),
        name="finish",
    )(old, chosen, head, grad, stay, far)


X, NEAR, FAR, CORE, Y = 1, 2, 4, 8, 16
GATHER = ((FAR, NEAR, X), (FAR, X, NEAR))
REDUCE = ((FAR, NEAR, Y, X), (FAR, X, NEAR, Y))


def span(basis):
    return [
        functools.reduce(lambda a, b: a ^ b, [m for k, m in enumerate(basis) if address >> k & 1], 0)
        for address in range(1 << len(basis))
    ]


ORDER, BLOCKS, LINES = 1, 17, 49


def tables():
    rows = []
    for level in range(2):
        for core in range(2):
            for place in range(8):
                halves, quarters = [], []
                for side in (core, 1 - core):
                    halves.append([2 * (place ^ m) + side for m in span(GATHER[side])])
                    quarters.append([4 * (place ^ m & 7) + 2 * side + (level ^ m >> 4) for m in span(REDUCE[side])])
                order = [h[lo : lo + 4] for lo in (0, 4) for h in halves]
                blocks = [q[lo : lo + 8] for lo in (8, 0) for q in quarters[::-1]]
                lines = [2 * (core ^ c) + (level ^ u) for c, u in ((0, 0), (0, 1), (1, 0), (1, 1))]
                rows.append([place] + sum(order, []) + sum(blocks, []) + lines)
    return np.array(rows, np.int32)


def swap(value, mask):
    masks = mask if isinstance(mask, tuple) else (mask, mask)
    shards, devices = lax.axis_size("fsdp"), lax.axis_size(AXES)
    return lax.ppermute(value, AXES, [(i, i ^ masks[i // shards & 1]) for i in range(devices)])


def local_cube(
    traj_hidden, traj_tokens, traj_action, traj_return, traj_episode,
    roll_hidden, roll_tokens, roll_action, station_table, norm_gain, head_weight,
):
    shard, actions = head_weight.shape
    half = shard // 2
    core = lax.axis_index("grp") % 2
    tab = lax.dynamic_index_in_dim(jnp.array(tables()), lax.axis_index(AXES), keepdims=False)

    wide = actions // 2
    held = [lax.dynamic_slice(head_weight, (core * half, c * wide), (half, wide))[None] for c in range(2)]
    came = [None, None]
    for k in range(3):
        for c in range(2):
            came[c] = swap(held[c], tuple(g[k] for g in GATHER))
            if k < 2:
                held[c] = jnp.concatenate([held[c], came[c]], axis=0)
    other_held, other_came = [], []
    for c in range(2):
        other_held.append(swap(held[c], CORE))
        other_came.append(swap(came[c], CORE))

    so_far, start, tall = (), 0, traj_hidden.shape[0]
    for rows in (tall * 3 // 8, tall * 3 // 8, tall // 4):
        so_far = features_call(
            shard, tab, start, rows, tuple(so_far), traj_hidden, roll_hidden, station_table,
            traj_tokens.reshape(1, -1), roll_tokens.reshape(1, -1), norm_gain.reshape(1, -1),
            traj_return.reshape(1, -1), traj_episode, traj_action.reshape(1, -1),
        )
        start += rows
    features, turned, roll_blocks, roll_parts, advantage, chosen = so_far
    logits = logits_call(features, tab, ORDER, [held, other_held])
    logits = logits_call(features, tab, ORDER + 8, [came], acc=logits)
    scores = logits_call(features, tab, ORDER + 12, [other_came], acc=logits, last=(advantage, chosen))

    crossed = []
    for part in range(2):
        outs = grad_call(scores, turned, tab, BLOCKS + 16 * part, 8, BF16)
        crossed.append([swap(out, CORE) for out in outs])
    sends = grad_call(scores, turned, tab, BLOCKS + 8, 8, BF16, *crossed[0])
    came_back = []
    for c in range(2):
        came_back.append(swap(sends[c], tuple(r[3] for r in REDUCE)))
    keeps = grad_call(scores, turned, tab, BLOCKS + 24, 8, F32, *crossed[1])
    parts = [[keeps[c], came_back[c]] for c in range(2)]
    for k in (2, 1, 0):
        n = 1 << k
        for c in range(2):
            send = sum(t[n : 2 * n].astype(F32) for t in parts[c]).astype(BF16)
            parts[c] = [t[:n] for t in parts[c]] + [swap(send, tuple(r[k] for r in REDUCE))]
    own = jnp.concatenate([sum(t.astype(F32) for t in p) for p in parts], axis=2).astype(BF16)
    lines = [own]
    for k, mask in enumerate((Y, CORE, CORE | Y)):
        lines.append(swap(own, mask))

    rolls = [roll_parts[0:1]]
    for m in range(1, 8):
        rolls.append(swap(roll_parts[m : m + 1], m))
    grad, *shares = share_call(tab, lines, rolls)
    for m in range(1, 4):
        shares[m] = swap(shares[m], m)
    stay, send = join_call(shares)
    far = swap(send, FAR)
    old = old_logits_call(roll_blocks, tab, [held, other_held, came, other_came])
    picked = (roll_action[:, None] == jnp.arange(actions, dtype=I32)[None, :]).astype(F32)
    new_head, action_logp, episode_logp = finish_call(old, picked, head_weight, grad.reshape(shard, actions), stay, far)
    return new_head, action_logp.reshape(-1), episode_logp.reshape(-1)


def station_rows(hidden, tokens, table, gain):
    stations = table.shape[0]
    lookup = (tokens[:, None] == jnp.arange(stations, dtype=I32)[None, :]).astype(BF16)
    embedded = jnp.dot(lookup, table, preferred_element_type=F32)
    mixed = hidden.astype(F32) + embedded
    power = jnp.mean(mixed * mixed, axis=-1, keepdims=True)
    return (mixed * lax.rsqrt(power + 1e-05) * gain).astype(BF16)


def picked_logp(logits, actions):
    top = jnp.max(logits, axis=-1, keepdims=True)
    total = jnp.log(jnp.sum(jnp.exp(logits - top), axis=-1)) + top[:, 0]
    chosen = (actions[:, None] == jnp.arange(logits.shape[1], dtype=I32)[None, :]).astype(F32)
    return jnp.sum(logits * chosen, axis=-1) - total


def episode_advantage(returns, episode):
    member = (episode[:, None] == jnp.arange(EPI_BLK, dtype=I32)[None, :]).astype(F32)
    sums = jnp.dot(member.T, returns, precision=lax.Precision.HIGHEST)
    counts = jnp.sum(member, axis=0)
    baseline = jnp.dot(member, sums / counts, precision=lax.Precision.HIGHEST)
    return returns - baseline


def local_plain(
    traj_hidden, traj_tokens, traj_action, traj_return, traj_episode,
    roll_hidden, roll_tokens, roll_action, station_table, norm_gain, head_weight,
):
    shard, actions = head_weight.shape
    features = station_rows(traj_hidden, traj_tokens, station_table, norm_gain)
    rollout = station_rows(roll_hidden, roll_tokens, station_table, norm_gain)
    advantage = episode_advantage(traj_return, traj_episode[0])
    full_old = lax.all_gather(head_weight, "fsdp", axis=0, tiled=True)
    logits = jnp.dot(features, full_old, preferred_element_type=F32)
    top = jnp.max(logits, axis=-1, keepdims=True)
    expo = jnp.exp(logits - top)
    probs = expo / jnp.sum(expo, axis=-1, keepdims=True)
    chosen = (traj_action[:, None] == jnp.arange(actions, dtype=I32)[None, :]).astype(F32)
    scores = (advantage[:, None] * (probs - chosen)).astype(BF16)
    local_grad = lax.dot_general(features, scores, (((0,), (0,)), ((), ())), preferred_element_type=F32)
    grad = lax.psum(local_grad, AXES)
    gnorm = jnp.sqrt(jnp.sum(grad * grad) + 1e-06)
    new_full = (full_old.astype(F32) - step_length * grad / gnorm).astype(BF16)
    new_head = lax.dynamic_slice_in_dim(new_full, lax.axis_index("fsdp") * shard, shard, 0)
    roll_logits = jnp.dot(rollout, new_full, preferred_element_type=F32)
    action_logp = picked_logp(roll_logits, roll_action)
    return new_head, action_logp, jnp.sum(action_logp.reshape(-1, STEPS), axis=1)


def fits(args, groups, shards):
    hidden, episode, roll, table, head = args[0], args[4], args[5], args[8], args[10]
    if (groups, shards) != (4, 8) or episode.shape[0] != 1:
        return False
    aligned = head.shape[0] % 512 == 0 and head.shape[1] % 128 == 0 and table.shape[0] % 128 == 0
    whole = hidden.shape[1] == shards * head.shape[0] and hidden.shape[0] % 1024 == 0
    return aligned and whole and roll.shape[0] <= 128 and roll.shape[0] % STEPS == 0


def solution(mesh):
    groups, shards = mesh.shape["grp"], mesh.shape["fsdp"]

    def local(*args):
        if not fits(args, groups, shards):
            return local_plain(*args)
        return local_cube(*args)

    both = P(AXES)
    wide = P(AXES, None)
    return jax.shard_map(
        local,
        mesh=mesh,
        in_specs=(wide, both, both, both, wide, wide, both, both, P(), P(), P("fsdp", None)),
        out_specs=(P("fsdp", None), both, both),
        check_vma=False,
    )
```

```python
import functools

import jax
import jax.numpy as jnp
import numpy as np
from jax import lax
from jax.experimental import pallas as pl
from jax.experimental.pallas import tpu as pltpu
from jax.sharding import PartitionSpec as P


EPI_BLK = 8
STEPS = 64
AXES = ("grp", "fsdp")
F32, BF16, I32 = jnp.float32, jnp.bfloat16, jnp.int32

step_length = 8.0


def room(mib):
    return pltpu.CompilerParams(vmem_limit_bytes=mib << 20)


def column(row):
    blocks = [jnp.broadcast_to(row[:, at : at + 128], (128, 128)) for at in range(0, row.shape[1], 128)]
    return jnp.concatenate([jnp.transpose(b) for b in blocks], axis=0)


SLOTS = 4
FOOT = 8


def features_kernel(start, last, tab_ref, hidden_ref, roll_ref, table_ref, *refs):
    small = [pltpu.make_async_copy(refs[k], refs[k - 7], refs[-1].at[k]) for k in range(6)]
    token_ref, roll_token_ref, gain_ref, return_ref, episode_ref, action_ref = refs[-7:-1]
    lookup_ref, mixed_ref, feats_stage, turned_stage, hidden_slots, roll_slots, table_slots, sems, out_sems = refs[-16:-7]
    outs = refs[6 + (2 if start else 0) : -16]
    feats_ref, turned_ref = outs[:2]
    rows, wide = hidden_slots.shape[1:]
    few, half, chunks = roll_slots.shape[1], wide // 2, mixed_ref.shape[0]
    groups = [(0, rows, hidden_slots)] + ([(rows, few, roll_slots)] if last else [])

    def fetch(chunk):
        slot, cut = chunk % SLOTS, slice(chunk * wide, (chunk + 1) * wide)
        moves = [(hidden_ref.at[start : start + rows, cut], hidden_slots), (table_ref.at[:, cut], table_slots)]
        if last:
            moves.append((roll_ref.at[:, cut], roll_slots))
        return [
            pltpu.make_async_copy(source, slots.at[slot], sems.at[k, slot]) for k, (source, slots) in enumerate(moves)
        ]

    def flush(chunk):
        slot = chunk % 2
        to = feats_ref.at[2 * chunk : 2 * chunk + 2, start : start + rows, :]
        turned_to = turned_ref.at[4 * chunk : 4 * chunk + 4, :, start : start + rows]
        return [
            pltpu.make_async_copy(feats_stage.at[slot], to, out_sems.at[0, slot]),
            pltpu.make_async_copy(turned_stage.at[slot], turned_to, out_sems.at[1, slot]),
        ]

    for copy in small:
        copy.start()
    for chunk in range(min(SLOTS, chunks)):
        for copy in fetch(chunk):
            copy.start()
    for copy in small:
        copy.wait()
    down = column(token_ref[:, start : start + rows])
    if last:
        here = lax.broadcasted_iota(I32, (few, few), 0) == lax.broadcasted_iota(I32, (few, few), 1)
        end = jnp.sum(jnp.where(here, roll_token_ref[...].astype(F32), 0.0), axis=1, keepdims=True).astype(I32)
        down = jnp.concatenate([down, jnp.broadcast_to(end, (few, 128))], axis=0)
    lane = lax.broadcasted_iota(I32, down.shape, 1)
    for at in range(0, table_ref.shape[0], 128):
        lookup_ref[:, at : at + 128] = jnp.where(down == lane + at, 1.0, 0.0).astype(BF16)
    powers = [jnp.zeros((n, 128), F32) for _, n, _ in groups]
    for chunk in range(chunks):
        slot = chunk % SLOTS
        for copy in fetch(chunk):
            copy.wait()
        embedded = jnp.dot(lookup_ref[...], table_slots[slot], preferred_element_type=F32)
        for g, (lo, n, ref) in enumerate(groups):
            mixed = ref[slot].astype(F32) + embedded[lo : lo + n]
            mixed_ref[chunk, lo : lo + n] = mixed
            square = mixed * mixed
            for at in range(0, wide, 128):
                powers[g] = powers[g] + square[:, at : at + 128]
        if chunk + SLOTS < chunks:
            for copy in fetch(chunk + SLOTS):
                copy.start()
    if last:
        returns, episode = return_ref[...], episode_ref[...]
        baseline = jnp.zeros_like(returns)
        for e in range(EPI_BLK):
            member = episode == e
            total = jnp.sum(jnp.where(member, returns, 0.0), axis=-1, keepdims=True)
            count = jnp.sum(jnp.where(member, 1.0, 0.0), axis=-1, keepdims=True)
            baseline = jnp.where(member, total / jnp.maximum(count, 1.0), baseline)
        outs[4][...] = column(returns - baseline)
        outs[5][...] = column(action_ref[...])
    scales = [lax.rsqrt(jnp.sum(p, axis=-1, keepdims=True) / (chunks * wide) + 1e-05) for p in powers]
    for chunk in range(chunks):
        slot, cut = chunk % 2, slice(chunk * wide, (chunk + 1) * wide)
        if chunk >= 2:
            for copy in flush(chunk - 2):
                copy.wait()
        value = (mixed_ref[chunk, :rows] * scales[0] * gain_ref[:, cut]).astype(BF16)
        feats_stage[slot, 0], feats_stage[slot, 1] = value[:, :half], value[:, half:]
        turned_stage[slot] = jnp.transpose(value).reshape(turned_stage.shape[1:])
        for copy in flush(chunk):
            copy.start()
        if last:
            value = (mixed_ref[chunk, rows:] * scales[1] * gain_ref[:, cut]).astype(BF16)
            roll_out_ref, roll_rel_ref = outs[2:4]
            roll_out_ref[2 * chunk], roll_out_ref[2 * chunk + 1] = value[:, :half], value[:, half:]
            roll_rel_ref[jnp.bitwise_xor(tab_ref[0], chunk)] = value
    for chunk in range(max(chunks - 2, 0), chunks):
        for copy in flush(chunk):
            copy.wait()


def features_call(shard, tab, start, rows, so_far, hidden, roll, table, tokens, roll_tokens, gain, returns, episode, action):
    tall, width = hidden.shape
    last = start + rows == tall
    half, few, chunks = shard // 2, roll.shape[0], width // shard
    quarter, all_rows = half // 2, rows + (few if last else 0)
    hbm, vmem = pl.BlockSpec(memory_space=pltpu.HBM), pl.BlockSpec(memory_space=pltpu.VMEM)
    anywhere = pl.BlockSpec(memory_space=pl.ANY)
    out_shape = [
        jax.ShapeDtypeStruct((2 * chunks, tall, half), BF16),
        jax.ShapeDtypeStruct((4 * chunks, quarter, tall), BF16),
        jax.ShapeDtypeStruct((2 * chunks, few, half), BF16),
        jax.ShapeDtypeStruct((chunks, few, shard), BF16),
        jax.ShapeDtypeStruct((tall, 128), F32),
        jax.ShapeDtypeStruct((tall, 128), I32),
    ]
    outs = 6 if last else 2
    args = (hidden, roll, table, tokens, roll_tokens, gain, returns, episode, action)
    args = [pltpu.with_memory_space_constraint(v, pltpu.HBM) for v in args]
    return pl.pallas_call(
        functools.partial(features_kernel, start, last),
        in_specs=[pl.BlockSpec(memory_space=pltpu.SMEM)] + [hbm] * 9 + [anywhere] * len(so_far),
        out_specs=([anywhere] * 2 + [vmem] * 4)[:outs],
        scratch_shapes=[
            pltpu.VMEM((all_rows, table.shape[0]), BF16),
            pltpu.VMEM((chunks, all_rows, shard), F32),
            pltpu.VMEM((2, 2, rows, half), BF16),
            pltpu.VMEM((2, 4, quarter, rows), BF16),
            pltpu.VMEM((SLOTS, rows, shard), BF16),
            pltpu.VMEM((SLOTS, few, shard), BF16),
            pltpu.VMEM((SLOTS, table.shape[0], shard), BF16),
            pltpu.SemaphoreType.DMA((3, SLOTS)),
            pltpu.SemaphoreType.DMA((2, 2)),
        ]
        + [pltpu.VMEM(v.shape, v.dtype) for v in args[3:]]
        + [pltpu.SemaphoreType.DMA((6,))],
        out_shape=out_shape[:outs],
        input_output_aliases={10 + k: k for k in range(len(so_far))},
        cost_estimate=pl.CostEstimate(
            flops=4 * rows * width * table.shape[0], transcendentals=0, bytes_accessed=8 * rows * width
        ),
        compiler_params=room(24),
        name="features",
    )(tab, *args, *so_far)


def join_heads(refs, pieces):
    halves = [
        jnp.concatenate([ref[p] for ref, n in zip(refs[c::2], pieces) for p in range(n)], axis=0) for c in range(2)
    ]
    return jnp.concatenate(halves, axis=1)


def logits_kernel(pieces, has_acc, last, tab_ref, *refs):
    count = sum(pieces)
    feats, refs = refs[:count], refs[count:]
    heads, refs = refs[: 2 * len(pieces)], refs[2 * len(pieces) :]
    left = jnp.concatenate([ref[0] for ref in feats], axis=1)
    right = join_heads(heads, pieces)
    logits = jnp.dot(left, right, preferred_element_type=F32)
    if has_acc:
        logits = logits + refs[0][...]
        refs = refs[1:]
    if not last:
        refs[0][...] = logits
        return
    advantage_ref, chosen_ref, out_ref = refs
    actions = logits.shape[1]
    top = jnp.max(logits, axis=1, keepdims=True)
    expo = jnp.exp(logits - top)
    probs = expo / jnp.sum(expo, axis=1, keepdims=True)
    advantage, action = advantage_ref[...], chosen_ref[...]
    lane = lax.broadcasted_iota(I32, action.shape, 1)
    for at in range(0, actions, 128):
        chosen = jnp.where(action == lane + at, 1.0, 0.0)
        out_ref[:, at : at + 128] = (advantage * (probs[:, at : at + 128] - chosen)).astype(BF16)


def logits_call(feats, tab, at, heads, acc=None, last=None):
    _, rows, half = feats.shape
    actions = 2 * heads[0][0].shape[2]
    pieces = tuple(h[0].shape[0] for h in heads)
    heads = [h for pair in heads for h in pair]
    count = sum(pieces)
    tall = 512
    block = pl.BlockSpec((tall, actions), lambda i, t: (i, 0))
    thin = pl.BlockSpec((tall, 128), lambda i, t: (i, 0))
    in_specs = [
        pl.BlockSpec((1, tall, half), functools.partial(lambda k, i, t: (t[k], i, 0), at + k)) for k in range(count)
    ]
    in_specs += [pl.BlockSpec(h.shape, lambda i, t: (0, 0, 0)) for h in heads]
    args = [feats] * count + list(heads)
    if acc is not None:
        in_specs.append(block)
        args.append(acc)
    if last is not None:
        in_specs += [thin, thin]
        args += list(last)
    return pl.pallas_call(
        functools.partial(logits_kernel, pieces, acc is not None, last is not None),
        grid_spec=pltpu.PrefetchScalarGridSpec(
            num_scalar_prefetch=1, grid=(rows // tall,), in_specs=in_specs, out_specs=block
        ),
        out_shape=jax.ShapeDtypeStruct((rows, actions), F32 if last is None else BF16),
        cost_estimate=pl.CostEstimate(
            flops=2 * rows * count * half * actions, transcendentals=0, bytes_accessed=2 * rows * count * half
        ),
        compiler_params=room(12),
        name="logits",
    )(tab, *args)


def grad_kernel(count, tab_ref, scores_ref, *refs):
    feats, extra, outs = refs[:count], refs[count:-2], refs[-2:]
    left = jnp.concatenate([ref[0] for ref in feats], axis=0)
    wide = outs[0].shape[2]
    for c, out_ref in enumerate(outs):
        right = scores_ref[:, c * wide : (c + 1) * wide]
        out = jnp.dot(left, right, preferred_element_type=F32).reshape(out_ref.shape)
        if extra:
            out = out + extra[c][...].astype(F32)
        out_ref[...] = out.astype(out_ref.dtype)


def grad_call(scores, turned, tab, at, count, dtype, *extra):
    _, quarter, rows = turned.shape
    actions = scores.shape[1]
    each = min(count, 4)
    block = pl.BlockSpec((each, quarter, actions // 2), lambda i, t: (i, 0, 0))
    return pl.pallas_call(
        functools.partial(grad_kernel, each),
        grid_spec=pltpu.PrefetchScalarGridSpec(
            num_scalar_prefetch=1,
            grid=(count // each,),
            in_specs=[pl.BlockSpec((rows, actions), lambda i, t: (0, 0))]
            + [
                pl.BlockSpec((1, quarter, rows), functools.partial(lambda k, i, t: (t[at + i * each + k], 0, 0), k))
                for k in range(each)
            ]
            + [block] * len(extra),
            out_specs=[block] * 2,
        ),
        out_shape=[jax.ShapeDtypeStruct((count, quarter, actions // 2), dtype)] * 2,
        cost_estimate=pl.CostEstimate(
            flops=2 * rows * count * quarter * actions, transcendentals=0, bytes_accessed=2 * rows * count * quarter
        ),
        compiler_params=room(10),
        name="grad",
    )(tab, scores, *[turned] * each, *extra)


def old_logits_kernel(pieces, tab_ref, roll_ref, *refs):
    heads, out_ref = refs[:-1], refs[-1]
    left = jnp.concatenate([roll_ref[tab_ref[ORDER + k]] for k in range(sum(pieces))], axis=1)
    out_ref[...] = jnp.dot(left, join_heads(heads, pieces), preferred_element_type=F32)


def old_logits_call(roll, tab, heads):
    pieces = tuple(h[0].shape[0] for h in heads)
    heads = [h for pair in heads for h in pair]
    full = lambda shape: pl.BlockSpec(shape, lambda i, t: (0,) * len(shape))
    out = (roll.shape[1], 2 * heads[0].shape[2])
    return pl.pallas_call(
        functools.partial(old_logits_kernel, pieces),
        grid_spec=pltpu.PrefetchScalarGridSpec(
            num_scalar_prefetch=1,
            grid=(1,),
            in_specs=[full(roll.shape)] + [full(h.shape) for h in heads],
            out_specs=full(out),
        ),
        out_shape=jax.ShapeDtypeStruct(out, F32),
        compiler_params=room(12),
        name="old_logits",
    )(tab, roll, *heads)


def split(value, wide):
    first = value.astype(BF16).astype(F32)
    second = (value - first).astype(BF16).astype(F32)
    line = lax.broadcasted_iota(I32, (FOOT, wide), 0)
    third = jnp.where(line == 2, value - first - second, 0.0)
    return jnp.where(line == 0, first, jnp.where(line == 1, second, third)).astype(BF16)


def share_kernel(count, tab_ref, *refs):
    lines, rolls, grad_ref, outs = refs[:4], refs[4 : 4 + count], refs[4 + count], refs[5 + count :]
    quarter, actions = lines[0].shape[1:]
    for k, ref in enumerate(lines):
        grad_ref[tab_ref[LINES + k]] = ref[0]
    grad = grad_ref[...].reshape(4 * quarter, actions)
    wide = grad.astype(F32)
    square = jnp.sum(wide * wide, keepdims=True)
    rows = rolls[0].shape[1]
    left = jnp.concatenate([ref[0] for ref in rolls], axis=0)
    part = jnp.dot(left, grad, preferred_element_type=F32)
    foot = split(square, actions)
    far = count // 2
    for m in range(count):
        outs[m % far][m // far, :rows] = part[m * rows : (m + 1) * rows].astype(BF16)
        outs[m % far][m // far, rows:] = foot


def share_call(tab, lines, rolls):
    quarter, actions = lines[0].shape[1:]
    rows = rolls[0].shape[1]
    full = lambda shape: pl.BlockSpec(shape, lambda i, t: (0,) * len(shape))
    shape = (2, rows + FOOT, actions)
    return pl.pallas_call(
        functools.partial(share_kernel, len(rolls)),
        grid_spec=pltpu.PrefetchScalarGridSpec(
            num_scalar_prefetch=1,
            grid=(1,),
            in_specs=[full(lines[0].shape)] * 4 + [full(rolls[0].shape)] * len(rolls),
            out_specs=[full((4, quarter, actions))] + [full(shape)] * (len(rolls) // 2),
        ),
        out_shape=[jax.ShapeDtypeStruct((4, quarter, actions), BF16)]
        + [jax.ShapeDtypeStruct(shape, BF16)] * (len(rolls) // 2),
        compiler_params=room(6),
        name="share",
    )(tab, *lines, *rolls)


def join_kernel(*refs):
    parts, (stay_ref, send_ref) = refs[:-2], refs[-2:]
    rows = stay_ref.shape[0] - FOOT
    for k, out_ref in enumerate((stay_ref, send_ref)):
        total = parts[0][k].astype(F32)
        for ref in parts[1:]:
            total = total + ref[k].astype(F32)
        out_ref[:rows] = total[:rows].astype(out_ref.dtype)
        square = jnp.sum(total[rows:], axis=0, keepdims=True)
        if k == 0:
            out_ref[rows:] = jnp.broadcast_to(square, (FOOT, square.shape[1]))
        else:
            out_ref[rows:] = split(square, square.shape[1])


def join_call(parts):
    shape = parts[0].shape[1:]
    return pl.pallas_call(
        join_kernel,
        out_shape=[jax.ShapeDtypeStruct(shape, F32), jax.ShapeDtypeStruct(shape, BF16)],
        compiler_params=room(4),
        name="join",
    )(*parts)


def finish_kernel(old_ref, chosen_ref, head_ref, grad_ref, stay_ref, far_ref, head_out, logp_out, episode_out):
    rows, _ = old_ref.shape
    update = stay_ref[:rows] + far_ref[:rows].astype(F32)
    square = stay_ref[rows : rows + 1] + jnp.sum(far_ref[rows:].astype(F32), axis=0, keepdims=True)
    gnorm = jnp.sqrt(square + 1e-06)
    logits = old_ref[...] - step_length * update / gnorm
    top = jnp.max(logits, axis=-1, keepdims=True)
    total = jnp.log(jnp.sum(jnp.exp(logits - top), axis=-1, keepdims=True)) + top
    logp = jnp.sum(logits * chosen_ref[...], axis=-1, keepdims=True) - total
    here = lax.broadcasted_iota(I32, (rows, rows), 0) == lax.broadcasted_iota(I32, (rows, rows), 1)
    logp_out[...] = jnp.sum(jnp.where(here, logp, 0.0), axis=0, keepdims=True)
    episodes = rows // STEPS
    mine = lax.broadcasted_iota(I32, (rows, episodes), 0) // STEPS == lax.broadcasted_iota(I32, (rows, episodes), 1)
    episode_out[...] = jnp.sum(jnp.where(mine, logp, 0.0), axis=0, keepdims=True)
    head_out[...] = (head_ref[...].astype(F32) - step_length * grad_ref[...].astype(F32) / gnorm).astype(BF16)


def finish_call(old, chosen, head, grad, stay, far):
    rows = old.shape[0]
    return pl.pallas_call(
        finish_kernel,
        out_shape=[
            jax.ShapeDtypeStruct(head.shape, BF16),
            jax.ShapeDtypeStruct((1, rows), F32),
            jax.ShapeDtypeStruct((1, rows // STEPS), F32),
        ],
        compiler_params=room(6),
        name="finish",
    )(old, chosen, head, grad, stay, far)


X, NEAR, FAR, CORE, Y = 1, 2, 4, 8, 16
GATHER = ((FAR, NEAR, X), (FAR, X, NEAR))
REDUCE = ((FAR, NEAR, Y, X), (FAR, X, NEAR, Y))


def span(basis):
    return [
        functools.reduce(lambda a, b: a ^ b, [m for k, m in enumerate(basis) if address >> k & 1], 0)
        for address in range(1 << len(basis))
    ]


ORDER, BLOCKS, LINES = 1, 17, 49


def tables():
    rows = []
    for level in range(2):
        for core in range(2):
            for place in range(8):
                halves, quarters = [], []
                for side in (core, 1 - core):
                    halves.append([2 * (place ^ m) + side for m in span(GATHER[side])])
                    quarters.append([4 * (place ^ m & 7) + 2 * side + (level ^ m >> 4) for m in span(REDUCE[side])])
                order = [h[lo : lo + 4] for lo in (0, 4) for h in halves]
                blocks = [q[lo : lo + 8] for lo in (8, 0) for q in quarters[::-1]]
                lines = [2 * (core ^ c) + (level ^ u) for c, u in ((0, 0), (0, 1), (1, 0), (1, 1))]
                rows.append([place] + sum(order, []) + sum(blocks, []) + lines)
    return np.array(rows, np.int32)


def swap(value, mask):
    masks = mask if isinstance(mask, tuple) else (mask, mask)
    shards, devices = lax.axis_size("fsdp"), lax.axis_size(AXES)
    return lax.ppermute(value, AXES, [(i, i ^ masks[i // shards & 1]) for i in range(devices)])


def local_cube(
    traj_hidden, traj_tokens, traj_action, traj_return, traj_episode,
    roll_hidden, roll_tokens, roll_action, station_table, norm_gain, head_weight,
):
    shard, actions = head_weight.shape
    half = shard // 2
    core = lax.axis_index("grp") % 2
    tab = lax.dynamic_index_in_dim(jnp.array(tables()), lax.axis_index(AXES), keepdims=False)

    wide = actions // 2
    held = [lax.dynamic_slice(head_weight, (core * half, c * wide), (half, wide))[None] for c in range(2)]
    came = [None, None]
    for k in range(3):
        for c in range(2):
            came[c] = swap(held[c], tuple(g[k] for g in GATHER))
            if k < 2:
                held[c] = jnp.concatenate([held[c], came[c]], axis=0)
    other_held, other_came = [], []
    for c in range(2):
        other_held.append(swap(held[c], CORE))
        other_came.append(swap(came[c], CORE))

    so_far, start, tall = (), 0, traj_hidden.shape[0]
    for rows in (tall // 2, tall // 4, tall // 4):
        so_far = features_call(
            shard, tab, start, rows, tuple(so_far), traj_hidden, roll_hidden, station_table,
            traj_tokens.reshape(1, -1), roll_tokens.reshape(1, -1), norm_gain.reshape(1, -1),
            traj_return.reshape(1, -1), traj_episode, traj_action.reshape(1, -1),
        )
        start += rows
    features, turned, roll_blocks, roll_parts, advantage, chosen = so_far
    logits = logits_call(features, tab, ORDER, [held, other_held])
    logits = logits_call(features, tab, ORDER + 8, [came], acc=logits)
    scores = logits_call(features, tab, ORDER + 12, [other_came], acc=logits, last=(advantage, chosen))

    crossed = []
    for part in range(2):
        outs = grad_call(scores, turned, tab, BLOCKS + 16 * part, 8, BF16)
        crossed.append([swap(out, CORE) for out in outs])
    sends = grad_call(scores, turned, tab, BLOCKS + 8, 8, BF16, *crossed[0])
    came_back = []
    for c in range(2):
        came_back.append(swap(sends[c], tuple(r[3] for r in REDUCE)))
    keeps = grad_call(scores, turned, tab, BLOCKS + 24, 8, F32, *crossed[1])
    parts = [[keeps[c], came_back[c]] for c in range(2)]
    for k in (2, 1, 0):
        n = 1 << k
        for c in range(2):
            send = sum(t[n : 2 * n].astype(F32) for t in parts[c]).astype(BF16)
            parts[c] = [t[:n] for t in parts[c]] + [swap(send, tuple(r[k] for r in REDUCE))]
    own = jnp.concatenate([sum(t.astype(F32) for t in p) for p in parts], axis=2).astype(BF16)
    lines = [own]
    for k, mask in enumerate((Y, CORE, CORE | Y)):
        lines.append(swap(own, mask))

    rolls = [roll_parts[0:1]]
    for m in range(1, 8):
        rolls.append(swap(roll_parts[m : m + 1], m))
    grad, *shares = share_call(tab, lines, rolls)
    for m in range(1, 4):
        shares[m] = swap(shares[m], m)
    stay, send = join_call(shares)
    far = swap(send, FAR)
    old = old_logits_call(roll_blocks, tab, [held, other_held, came, other_came])
    picked = (roll_action[:, None] == jnp.arange(actions, dtype=I32)[None, :]).astype(F32)
    new_head, action_logp, episode_logp = finish_call(old, picked, head_weight, grad.reshape(shard, actions), stay, far)
    return new_head, action_logp.reshape(-1), episode_logp.reshape(-1)


def station_rows(hidden, tokens, table, gain):
    stations = table.shape[0]
    lookup = (tokens[:, None] == jnp.arange(stations, dtype=I32)[None, :]).astype(BF16)
    embedded = jnp.dot(lookup, table, preferred_element_type=F32)
    mixed = hidden.astype(F32) + embedded
    power = jnp.mean(mixed * mixed, axis=-1, keepdims=True)
    return (mixed * lax.rsqrt(power + 1e-05) * gain).astype(BF16)


def picked_logp(logits, actions):
    top = jnp.max(logits, axis=-1, keepdims=True)
    total = jnp.log(jnp.sum(jnp.exp(logits - top), axis=-1)) + top[:, 0]
    chosen = (actions[:, None] == jnp.arange(logits.shape[1], dtype=I32)[None, :]).astype(F32)
    return jnp.sum(logits * chosen, axis=-1) - total


def episode_advantage(returns, episode):
    member = (episode[:, None] == jnp.arange(EPI_BLK, dtype=I32)[None, :]).astype(F32)
    sums = jnp.dot(member.T, returns, precision=lax.Precision.HIGHEST)
    counts = jnp.sum(member, axis=0)
    baseline = jnp.dot(member, sums / counts, precision=lax.Precision.HIGHEST)
    return returns - baseline


def local_plain(
    traj_hidden, traj_tokens, traj_action, traj_return, traj_episode,
    roll_hidden, roll_tokens, roll_action, station_table, norm_gain, head_weight,
):
    shard, actions = head_weight.shape
    features = station_rows(traj_hidden, traj_tokens, station_table, norm_gain)
    rollout = station_rows(roll_hidden, roll_tokens, station_table, norm_gain)
    advantage = episode_advantage(traj_return, traj_episode[0])
    full_old = lax.all_gather(head_weight, "fsdp", axis=0, tiled=True)
    logits = jnp.dot(features, full_old, preferred_element_type=F32)
    top = jnp.max(logits, axis=-1, keepdims=True)
    expo = jnp.exp(logits - top)
    probs = expo / jnp.sum(expo, axis=-1, keepdims=True)
    chosen = (traj_action[:, None] == jnp.arange(actions, dtype=I32)[None, :]).astype(F32)
    scores = (advantage[:, None] * (probs - chosen)).astype(BF16)
    local_grad = lax.dot_general(features, scores, (((0,), (0,)), ((), ())), preferred_element_type=F32)
    grad = lax.psum(local_grad, AXES)
    gnorm = jnp.sqrt(jnp.sum(grad * grad) + 1e-06)
    new_full = (full_old.astype(F32) - step_length * grad / gnorm).astype(BF16)
    new_head = lax.dynamic_slice_in_dim(new_full, lax.axis_index("fsdp") * shard, shard, 0)
    roll_logits = jnp.dot(rollout, new_full, preferred_element_type=F32)
    action_logp = picked_logp(roll_logits, roll_action)
    return new_head, action_logp, jnp.sum(action_logp.reshape(-1, STEPS), axis=1)


def fits(args, groups, shards):
    hidden, episode, roll, table, head = args[0], args[4], args[5], args[8], args[10]
    if (groups, shards) != (4, 8) or episode.shape[0] != 1:
        return False
    aligned = head.shape[0] % 512 == 0 and head.shape[1] % 128 == 0 and table.shape[0] % 128 == 0
    whole = hidden.shape[1] == shards * head.shape[0] and hidden.shape[0] % 1024 == 0
    return aligned and whole and roll.shape[0] <= 128 and roll.shape[0] % STEPS == 0


def solution(mesh):
    groups, shards = mesh.shape["grp"], mesh.shape["fsdp"]

    def local(*args):
        if not fits(args, groups, shards):
            return local_plain(*args)
        return local_cube(*args)

    both = P(AXES)
    wide = P(AXES, None)
    return jax.shard_map(
        local,
        mesh=mesh,
        in_specs=(wide, both, both, both, wide, wide, both, both, P(), P(), P("fsdp", None)),
        out_specs=(P("fsdp", None), both, both),
        check_vma=False,
    )
```

```python
import functools

import jax
import jax.numpy as jnp
import numpy as np
from jax import lax
from jax.experimental import pallas as pl
from jax.experimental.pallas import tpu as pltpu
from jax.sharding import PartitionSpec as P


EPI_BLK = 8
STEPS = 64
AXES = ("grp", "fsdp")
F32, BF16, I32 = jnp.float32, jnp.bfloat16, jnp.int32

step_length = 8.0


def room(mib):
    return pltpu.CompilerParams(vmem_limit_bytes=mib << 20)


def column(row):
    blocks = [jnp.broadcast_to(row[:, at : at + 128], (128, 128)) for at in range(0, row.shape[1], 128)]
    return jnp.concatenate([jnp.transpose(b) for b in blocks], axis=0)


SLOTS = 4
FOOT = 8


def features_kernel(start, last, tab_ref, hidden_ref, roll_ref, table_ref, *refs):
    small = [pltpu.make_async_copy(refs[k], refs[k - 7], refs[-1].at[k]) for k in range(6)]
    token_ref, roll_token_ref, gain_ref, return_ref, episode_ref, action_ref = refs[-7:-1]
    lookup_ref, mixed_ref, feats_stage, turned_stage, hidden_slots, roll_slots, table_slots, sems, out_sems = refs[-16:-7]
    outs = refs[6 + (2 if start else 0) : -16]
    feats_ref, turned_ref = outs[:2]
    rows, wide = hidden_slots.shape[1:]
    few, half, chunks = roll_slots.shape[1], wide // 2, mixed_ref.shape[0]
    groups = [(0, rows, hidden_slots)] + ([(rows, few, roll_slots)] if last else [])

    def fetch(chunk):
        slot, cut = chunk % SLOTS, slice(chunk * wide, (chunk + 1) * wide)
        moves = [(hidden_ref.at[start : start + rows, cut], hidden_slots), (table_ref.at[:, cut], table_slots)]
        if last:
            moves.append((roll_ref.at[:, cut], roll_slots))
        return [
            pltpu.make_async_copy(source, slots.at[slot], sems.at[k, slot]) for k, (source, slots) in enumerate(moves)
        ]

    def flush(chunk):
        slot = chunk % 2
        to = feats_ref.at[2 * chunk : 2 * chunk + 2, start : start + rows, :]
        turned_to = turned_ref.at[4 * chunk : 4 * chunk + 4, :, start : start + rows]
        return [
            pltpu.make_async_copy(feats_stage.at[slot], to, out_sems.at[0, slot]),
            pltpu.make_async_copy(turned_stage.at[slot], turned_to, out_sems.at[1, slot]),
        ]

    for copy in small:
        copy.start()
    for chunk in range(min(SLOTS, chunks)):
        for copy in fetch(chunk):
            copy.start()
    for copy in small:
        copy.wait()
    down = column(token_ref[:, start : start + rows])
    if last:
        here = lax.broadcasted_iota(I32, (few, few), 0) == lax.broadcasted_iota(I32, (few, few), 1)
        end = jnp.sum(jnp.where(here, roll_token_ref[...].astype(F32), 0.0), axis=1, keepdims=True).astype(I32)
        down = jnp.concatenate([down, jnp.broadcast_to(end, (few, 128))], axis=0)
    lane = lax.broadcasted_iota(I32, down.shape, 1)
    for at in range(0, table_ref.shape[0], 128):
        lookup_ref[:, at : at + 128] = jnp.where(down == lane + at, 1.0, 0.0).astype(BF16)
    powers = [jnp.zeros((n, 128), F32) for _, n, _ in groups]
    for chunk in range(chunks):
        slot = chunk % SLOTS
        for copy in fetch(chunk):
            copy.wait()
        embedded = jnp.dot(lookup_ref[...], table_slots[slot], preferred_element_type=F32)
        for g, (lo, n, ref) in enumerate(groups):
            mixed = ref[slot].astype(F32) + embedded[lo : lo + n]
            mixed_ref[chunk, lo : lo + n] = mixed
            square = mixed * mixed
            for at in range(0, wide, 128):
                powers[g] = powers[g] + square[:, at : at + 128]
        if chunk + SLOTS < chunks:
            for copy in fetch(chunk + SLOTS):
                copy.start()
    if last:
        returns, episode = return_ref[...], episode_ref[...]
        baseline = jnp.zeros_like(returns)
        for e in range(EPI_BLK):
            member = episode == e
            total = jnp.sum(jnp.where(member, returns, 0.0), axis=-1, keepdims=True)
            count = jnp.sum(jnp.where(member, 1.0, 0.0), axis=-1, keepdims=True)
            baseline = jnp.where(member, total / jnp.maximum(count, 1.0), baseline)
        outs[4][...] = column(returns - baseline)
        outs[5][...] = column(action_ref[...])
    scales = [lax.rsqrt(jnp.sum(p, axis=-1, keepdims=True) / (chunks * wide) + 1e-05) for p in powers]
    for chunk in range(chunks):
        slot, cut = chunk % 2, slice(chunk * wide, (chunk + 1) * wide)
        if chunk >= 2:
            for copy in flush(chunk - 2):
                copy.wait()
        value = (mixed_ref[chunk, :rows] * scales[0] * gain_ref[:, cut]).astype(BF16)
        feats_stage[slot, 0], feats_stage[slot, 1] = value[:, :half], value[:, half:]
        turned_stage[slot] = jnp.transpose(value).reshape(turned_stage.shape[1:])
        for copy in flush(chunk):
            copy.start()
        if last:
            value = (mixed_ref[chunk, rows:] * scales[1] * gain_ref[:, cut]).astype(BF16)
            roll_out_ref, roll_rel_ref = outs[2:4]
            roll_out_ref[2 * chunk], roll_out_ref[2 * chunk + 1] = value[:, :half], value[:, half:]
            roll_rel_ref[jnp.bitwise_xor(tab_ref[0], chunk)] = value
    for chunk in range(max(chunks - 2, 0), chunks):
        for copy in flush(chunk):
            copy.wait()


def features_call(shard, tab, start, rows, so_far, hidden, roll, table, tokens, roll_tokens, gain, returns, episode, action):
    tall, width = hidden.shape
    last = start + rows == tall
    half, few, chunks = shard // 2, roll.shape[0], width // shard
    quarter, all_rows = half // 2, rows + (few if last else 0)
    hbm, vmem = pl.BlockSpec(memory_space=pltpu.HBM), pl.BlockSpec(memory_space=pltpu.VMEM)
    anywhere = pl.BlockSpec(memory_space=pl.ANY)
    out_shape = [
        jax.ShapeDtypeStruct((2 * chunks, tall, half), BF16),
        jax.ShapeDtypeStruct((4 * chunks, quarter, tall), BF16),
        jax.ShapeDtypeStruct((2 * chunks, few, half), BF16),
        jax.ShapeDtypeStruct((chunks, few, shard), BF16),
        jax.ShapeDtypeStruct((tall, 128), F32),
        jax.ShapeDtypeStruct((tall, 128), I32),
    ]
    outs = 6 if last else 2
    args = (hidden, roll, table, tokens, roll_tokens, gain, returns, episode, action)
    args = [pltpu.with_memory_space_constraint(v, pltpu.HBM) for v in args]
    return pl.pallas_call(
        functools.partial(features_kernel, start, last),
        in_specs=[pl.BlockSpec(memory_space=pltpu.SMEM)] + [hbm] * 9 + [anywhere] * len(so_far),
        out_specs=([anywhere] * 2 + [vmem] * 4)[:outs],
        scratch_shapes=[
            pltpu.VMEM((all_rows, table.shape[0]), BF16),
            pltpu.VMEM((chunks, all_rows, shard), F32),
            pltpu.VMEM((2, 2, rows, half), BF16),
            pltpu.VMEM((2, 4, quarter, rows), BF16),
            pltpu.VMEM((SLOTS, rows, shard), BF16),
            pltpu.VMEM((SLOTS, few, shard), BF16),
            pltpu.VMEM((SLOTS, table.shape[0], shard), BF16),
            pltpu.SemaphoreType.DMA((3, SLOTS)),
            pltpu.SemaphoreType.DMA((2, 2)),
        ]
        + [pltpu.VMEM(v.shape, v.dtype) for v in args[3:]]
        + [pltpu.SemaphoreType.DMA((6,))],
        out_shape=out_shape[:outs],
        input_output_aliases={10 + k: k for k in range(len(so_far))},
        cost_estimate=pl.CostEstimate(
            flops=4 * rows * width * table.shape[0], transcendentals=0, bytes_accessed=8 * rows * width
        ),
        compiler_params=room(24),
        name="features",
    )(tab, *args, *so_far)


def join_heads(refs, pieces):
    halves = [
        jnp.concatenate([ref[p] for ref, n in zip(refs[c::2], pieces) for p in range(n)], axis=0) for c in range(2)
    ]
    return jnp.concatenate(halves, axis=1)


def logits_kernel(pieces, has_acc, last, tab_ref, *refs):
    count = sum(pieces)
    feats, refs = refs[:count], refs[count:]
    heads, refs = refs[: 2 * len(pieces)], refs[2 * len(pieces) :]
    left = jnp.concatenate([ref[0] for ref in feats], axis=1)
    right = join_heads(heads, pieces)
    logits = jnp.dot(left, right, preferred_element_type=F32)
    if has_acc:
        logits = logits + refs[0][...]
        refs = refs[1:]
    if not last:
        refs[0][...] = logits
        return
    advantage_ref, chosen_ref, out_ref = refs
    actions = logits.shape[1]
    top = jnp.max(logits, axis=1, keepdims=True)
    expo = jnp.exp(logits - top)
    probs = expo / jnp.sum(expo, axis=1, keepdims=True)
    advantage, action = advantage_ref[...], chosen_ref[...]
    lane = lax.broadcasted_iota(I32, action.shape, 1)
    for at in range(0, actions, 128):
        chosen = jnp.where(action == lane + at, 1.0, 0.0)
        out_ref[:, at : at + 128] = (advantage * (probs[:, at : at + 128] - chosen)).astype(BF16)


def logits_call(feats, tab, at, heads, acc=None, last=None):
    _, rows, half = feats.shape
    actions = 2 * heads[0][0].shape[2]
    pieces = tuple(h[0].shape[0] for h in heads)
    heads = [h for pair in heads for h in pair]
    count = sum(pieces)
    tall = 512
    block = pl.BlockSpec((tall, actions), lambda i, t: (i, 0))
    thin = pl.BlockSpec((tall, 128), lambda i, t: (i, 0))
    in_specs = [
        pl.BlockSpec((1, tall, half), functools.partial(lambda k, i, t: (t[k], i, 0), at + k)) for k in range(count)
    ]
    in_specs += [pl.BlockSpec(h.shape, lambda i, t: (0, 0, 0)) for h in heads]
    args = [feats] * count + list(heads)
    if acc is not None:
        in_specs.append(block)
        args.append(acc)
    if last is not None:
        in_specs += [thin, thin]
        args += list(last)
    return pl.pallas_call(
        functools.partial(logits_kernel, pieces, acc is not None, last is not None),
        grid_spec=pltpu.PrefetchScalarGridSpec(
            num_scalar_prefetch=1, grid=(rows // tall,), in_specs=in_specs, out_specs=block
        ),
        out_shape=jax.ShapeDtypeStruct((rows, actions), F32 if last is None else BF16),
        cost_estimate=pl.CostEstimate(
            flops=2 * rows * count * half * actions, transcendentals=0, bytes_accessed=2 * rows * count * half
        ),
        compiler_params=room(12),
        name="logits",
    )(tab, *args)


def grad_kernel(count, tab_ref, scores_ref, *refs):
    feats, extra, outs = refs[:count], refs[count:-2], refs[-2:]
    left = jnp.concatenate([ref[0] for ref in feats], axis=0)
    wide = outs[0].shape[2]
    for c, out_ref in enumerate(outs):
        right = scores_ref[:, c * wide : (c + 1) * wide]
        out = jnp.dot(left, right, preferred_element_type=F32).reshape(out_ref.shape)
        if extra:
            out = out + extra[c][...].astype(F32)
        out_ref[...] = out.astype(out_ref.dtype)


def grad_call(scores, turned, tab, at, count, dtype, *extra):
    _, quarter, rows = turned.shape
    actions = scores.shape[1]
    each = min(count, 4)
    block = pl.BlockSpec((each, quarter, actions // 2), lambda i, t: (i, 0, 0))
    return pl.pallas_call(
        functools.partial(grad_kernel, each),
        grid_spec=pltpu.PrefetchScalarGridSpec(
            num_scalar_prefetch=1,
            grid=(count // each,),
            in_specs=[pl.BlockSpec((rows, actions), lambda i, t: (0, 0))]
            + [
                pl.BlockSpec((1, quarter, rows), functools.partial(lambda k, i, t: (t[at + i * each + k], 0, 0), k))
                for k in range(each)
            ]
            + [block] * len(extra),
            out_specs=[block] * 2,
        ),
        out_shape=[jax.ShapeDtypeStruct((count, quarter, actions // 2), dtype)] * 2,
        cost_estimate=pl.CostEstimate(
            flops=2 * rows * count * quarter * actions, transcendentals=0, bytes_accessed=2 * rows * count * quarter
        ),
        compiler_params=room(10),
        name="grad",
    )(tab, scores, *[turned] * each, *extra)


def old_logits_kernel(pieces, tab_ref, roll_ref, *refs):
    heads, out_ref = refs[:-1], refs[-1]
    left = jnp.concatenate([roll_ref[tab_ref[ORDER + k]] for k in range(sum(pieces))], axis=1)
    out_ref[...] = jnp.dot(left, join_heads(heads, pieces), preferred_element_type=F32)


def old_logits_call(roll, tab, heads):
    pieces = tuple(h[0].shape[0] for h in heads)
    heads = [h for pair in heads for h in pair]
    full = lambda shape: pl.BlockSpec(shape, lambda i, t: (0,) * len(shape))
    out = (roll.shape[1], 2 * heads[0].shape[2])
    return pl.pallas_call(
        functools.partial(old_logits_kernel, pieces),
        grid_spec=pltpu.PrefetchScalarGridSpec(
            num_scalar_prefetch=1,
            grid=(1,),
            in_specs=[full(roll.shape)] + [full(h.shape) for h in heads],
            out_specs=full(out),
        ),
        out_shape=jax.ShapeDtypeStruct(out, F32),
        compiler_params=room(12),
        name="old_logits",
    )(tab, roll, *heads)


def split(value, wide):
    first = value.astype(BF16).astype(F32)
    second = (value - first).astype(BF16).astype(F32)
    line = lax.broadcasted_iota(I32, (FOOT, wide), 0)
    third = jnp.where(line == 2, value - first - second, 0.0)
    return jnp.where(line == 0, first, jnp.where(line == 1, second, third)).astype(BF16)


def share_kernel(count, tab_ref, *refs):
    lines, rolls, grad_ref, outs = refs[:3], refs[3 : 3 + count], refs[3 + count], refs[4 + count :]
    quarter, actions = lines[0].shape[1:]
    for k, (ref, at) in enumerate(((lines[0], 0), (lines[1], 0), (lines[2], 0), (lines[2], 1))):
        grad_ref[tab_ref[LINES + k]] = ref[at]
    grad = grad_ref[...].reshape(4 * quarter, actions)
    wide = grad.astype(F32)
    square = jnp.sum(wide * wide, keepdims=True)
    rows = rolls[0].shape[1]
    left = jnp.concatenate([ref[0] for ref in rolls], axis=0)
    part = jnp.dot(left, grad, preferred_element_type=F32)
    foot = split(square, actions)
    far = count // 2
    for m in range(count):
        outs[m % far][m // far, :rows] = part[m * rows : (m + 1) * rows].astype(BF16)
        outs[m % far][m // far, rows:] = foot


def share_call(tab, lines, rolls):
    quarter, actions = lines[0].shape[1:]
    rows = rolls[0].shape[1]
    full = lambda shape: pl.BlockSpec(shape, lambda i, t: (0,) * len(shape))
    shape = (2, rows + FOOT, actions)
    return pl.pallas_call(
        functools.partial(share_kernel, len(rolls)),
        grid_spec=pltpu.PrefetchScalarGridSpec(
            num_scalar_prefetch=1,
            grid=(1,),
            in_specs=[full(v.shape) for v in (*lines, *rolls)],
            out_specs=[full((4, quarter, actions))] + [full(shape)] * (len(rolls) // 2),
        ),
        out_shape=[jax.ShapeDtypeStruct((4, quarter, actions), BF16)]
        + [jax.ShapeDtypeStruct(shape, BF16)] * (len(rolls) // 2),
        compiler_params=room(6),
        name="share",
    )(tab, *lines, *rolls)


def join_kernel(*refs):
    parts, (stay_ref, send_ref) = refs[:-2], refs[-2:]
    rows = stay_ref.shape[0] - FOOT
    for k, out_ref in enumerate((stay_ref, send_ref)):
        total = parts[0][k].astype(F32)
        for ref in parts[1:]:
            total = total + ref[k].astype(F32)
        out_ref[:rows] = total[:rows].astype(out_ref.dtype)
        square = jnp.sum(total[rows:], axis=0, keepdims=True)
        if k == 0:
            out_ref[rows:] = jnp.broadcast_to(square, (FOOT, square.shape[1]))
        else:
            out_ref[rows:] = split(square, square.shape[1])


def join_call(parts):
    shape = parts[0].shape[1:]
    return pl.pallas_call(
        join_kernel,
        out_shape=[jax.ShapeDtypeStruct(shape, F32), jax.ShapeDtypeStruct(shape, BF16)],
        compiler_params=room(4),
        name="join",
    )(*parts)


def finish_kernel(old_ref, chosen_ref, head_ref, grad_ref, stay_ref, far_ref, head_out, logp_out, episode_out):
    rows, _ = old_ref.shape
    update = stay_ref[:rows] + far_ref[:rows].astype(F32)
    square = stay_ref[rows : rows + 1] + jnp.sum(far_ref[rows:].astype(F32), axis=0, keepdims=True)
    gnorm = jnp.sqrt(square + 1e-06)
    logits = old_ref[...] - step_length * update / gnorm
    top = jnp.max(logits, axis=-1, keepdims=True)
    total = jnp.log(jnp.sum(jnp.exp(logits - top), axis=-1, keepdims=True)) + top
    logp = jnp.sum(logits * chosen_ref[...], axis=-1, keepdims=True) - total
    here = lax.broadcasted_iota(I32, (rows, rows), 0) == lax.broadcasted_iota(I32, (rows, rows), 1)
    logp_out[...] = jnp.sum(jnp.where(here, logp, 0.0), axis=0, keepdims=True)
    episodes = rows // STEPS
    mine = lax.broadcasted_iota(I32, (rows, episodes), 0) // STEPS == lax.broadcasted_iota(I32, (rows, episodes), 1)
    episode_out[...] = jnp.sum(jnp.where(mine, logp, 0.0), axis=0, keepdims=True)
    head_out[...] = (head_ref[...].astype(F32) - step_length * grad_ref[...].astype(F32) / gnorm).astype(BF16)


def finish_call(old, chosen, head, grad, stay, far):
    rows = old.shape[0]
    return pl.pallas_call(
        finish_kernel,
        out_shape=[
            jax.ShapeDtypeStruct(head.shape, BF16),
            jax.ShapeDtypeStruct((1, rows), F32),
            jax.ShapeDtypeStruct((1, rows // STEPS), F32),
        ],
        compiler_params=room(6),
        name="finish",
    )(old, chosen, head, grad, stay, far)


X, NEAR, FAR, CORE, Y = 1, 2, 4, 8, 16
GATHER = ((FAR, NEAR, X), (FAR, X, NEAR))
REDUCE = ((FAR, NEAR, Y, X), (FAR, X, NEAR, Y))


def span(basis):
    return [
        functools.reduce(lambda a, b: a ^ b, [m for k, m in enumerate(basis) if address >> k & 1], 0)
        for address in range(1 << len(basis))
    ]


ORDER, BLOCKS, LINES = 1, 17, 49


def tables():
    rows = []
    for level in range(2):
        for core in range(2):
            for place in range(8):
                halves, quarters = [], []
                for side in (core, 1 - core):
                    halves.append([2 * (place ^ m) + side for m in span(GATHER[side])])
                    quarters.append([4 * (place ^ m & 7) + 2 * side + (level ^ m >> 4) for m in span(REDUCE[side])])
                order = [h[lo : lo + 4] for lo in (0, 4) for h in halves]
                blocks = [q[lo : lo + 8] for lo in (8, 0) for q in quarters[::-1]]
                lines = [2 * (core ^ c) + (level ^ u) for c, u in ((0, 0), (0, 1), (1, 0), (1, 1))]
                rows.append([place] + sum(order, []) + sum(blocks, []) + lines)
    return np.array(rows, np.int32)


def swap(value, mask):
    masks = mask if isinstance(mask, tuple) else (mask, mask)
    shards, devices = lax.axis_size("fsdp"), lax.axis_size(AXES)
    return lax.ppermute(value, AXES, [(i, i ^ masks[i // shards & 1]) for i in range(devices)])


def local_cube(
    traj_hidden, traj_tokens, traj_action, traj_return, traj_episode,
    roll_hidden, roll_tokens, roll_action, station_table, norm_gain, head_weight,
):
    shard, actions = head_weight.shape
    half = shard // 2
    core = lax.axis_index("grp") % 2
    tab = lax.dynamic_index_in_dim(jnp.array(tables()), lax.axis_index(AXES), keepdims=False)

    wide = actions // 2
    held = [lax.dynamic_slice(head_weight, (core * half, c * wide), (half, wide))[None] for c in range(2)]
    came = [None, None]
    for k in range(3):
        for c in range(2):
            came[c] = swap(held[c], tuple(g[k] for g in GATHER))
            if k < 2:
                held[c] = jnp.concatenate([held[c], came[c]], axis=0)
    other_held, other_came = [], []
    for c in range(2):
        other_held.append(swap(held[c], CORE))
        other_came.append(swap(came[c], CORE))

    so_far, start, tall = (), 0, traj_hidden.shape[0]
    for rows in (tall // 2, tall // 4, tall // 4):
        so_far = features_call(
            shard, tab, start, rows, tuple(so_far), traj_hidden, roll_hidden, station_table,
            traj_tokens.reshape(1, -1), roll_tokens.reshape(1, -1), norm_gain.reshape(1, -1),
            traj_return.reshape(1, -1), traj_episode, traj_action.reshape(1, -1),
        )
        start += rows
    features, turned, roll_blocks, roll_parts, advantage, chosen = so_far
    logits = logits_call(features, tab, ORDER, [held, other_held])
    logits = logits_call(features, tab, ORDER + 8, [came], acc=logits)
    scores = logits_call(features, tab, ORDER + 12, [other_came], acc=logits, last=(advantage, chosen))

    crossed = []
    for part in range(2):
        outs = grad_call(scores, turned, tab, BLOCKS + 16 * part, 8, BF16)
        crossed.append([swap(out, CORE) for out in outs])
    sends = grad_call(scores, turned, tab, BLOCKS + 8, 8, BF16, *crossed[0])
    came_back = []
    for c in range(2):
        came_back.append(swap(sends[c], tuple(r[3] for r in REDUCE)))
    keeps = grad_call(scores, turned, tab, BLOCKS + 24, 8, F32, *crossed[1])
    parts = [[keeps[c], came_back[c]] for c in range(2)]
    for k in (2, 1, 0):
        n = 1 << k
        for c in range(2):
            send = sum(t[n : 2 * n].astype(F32) for t in parts[c]).astype(BF16)
            parts[c] = [t[:n] for t in parts[c]] + [swap(send, tuple(r[k] for r in REDUCE))]
    own = jnp.concatenate([sum(t.astype(F32) for t in p) for p in parts], axis=2).astype(BF16)
    level = swap(own, Y)
    lines = [own, level, swap(jnp.concatenate([own, level], axis=0), CORE)]

    rolls = [roll_parts[0:1]]
    for m in range(1, 8):
        rolls.append(swap(roll_parts[m : m + 1], m))
    grad, *shares = share_call(tab, lines, rolls)
    for m in range(1, 4):
        shares[m] = swap(shares[m], m)
    stay, send = join_call(shares)
    far = swap(send, FAR)
    old = old_logits_call(roll_blocks, tab, [held, other_held, came, other_came])
    picked = (roll_action[:, None] == jnp.arange(actions, dtype=I32)[None, :]).astype(F32)
    new_head, action_logp, episode_logp = finish_call(old, picked, head_weight, grad.reshape(shard, actions), stay, far)
    return new_head, action_logp.reshape(-1), episode_logp.reshape(-1)


def station_rows(hidden, tokens, table, gain):
    stations = table.shape[0]
    lookup = (tokens[:, None] == jnp.arange(stations, dtype=I32)[None, :]).astype(BF16)
    embedded = jnp.dot(lookup, table, preferred_element_type=F32)
    mixed = hidden.astype(F32) + embedded
    power = jnp.mean(mixed * mixed, axis=-1, keepdims=True)
    return (mixed * lax.rsqrt(power + 1e-05) * gain).astype(BF16)


def picked_logp(logits, actions):
    top = jnp.max(logits, axis=-1, keepdims=True)
    total = jnp.log(jnp.sum(jnp.exp(logits - top), axis=-1)) + top[:, 0]
    chosen = (actions[:, None] == jnp.arange(logits.shape[1], dtype=I32)[None, :]).astype(F32)
    return jnp.sum(logits * chosen, axis=-1) - total


def episode_advantage(returns, episode):
    member = (episode[:, None] == jnp.arange(EPI_BLK, dtype=I32)[None, :]).astype(F32)
    sums = jnp.dot(member.T, returns, precision=lax.Precision.HIGHEST)
    counts = jnp.sum(member, axis=0)
    baseline = jnp.dot(member, sums / counts, precision=lax.Precision.HIGHEST)
    return returns - baseline


def local_plain(
    traj_hidden, traj_tokens, traj_action, traj_return, traj_episode,
    roll_hidden, roll_tokens, roll_action, station_table, norm_gain, head_weight,
):
    shard, actions = head_weight.shape
    features = station_rows(traj_hidden, traj_tokens, station_table, norm_gain)
    rollout = station_rows(roll_hidden, roll_tokens, station_table, norm_gain)
    advantage = episode_advantage(traj_return, traj_episode[0])
    full_old = lax.all_gather(head_weight, "fsdp", axis=0, tiled=True)
    logits = jnp.dot(features, full_old, preferred_element_type=F32)
    top = jnp.max(logits, axis=-1, keepdims=True)
    expo = jnp.exp(logits - top)
    probs = expo / jnp.sum(expo, axis=-1, keepdims=True)
    chosen = (traj_action[:, None] == jnp.arange(actions, dtype=I32)[None, :]).astype(F32)
    scores = (advantage[:, None] * (probs - chosen)).astype(BF16)
    local_grad = lax.dot_general(features, scores, (((0,), (0,)), ((), ())), preferred_element_type=F32)
    grad = lax.psum(local_grad, AXES)
    gnorm = jnp.sqrt(jnp.sum(grad * grad) + 1e-06)
    new_full = (full_old.astype(F32) - step_length * grad / gnorm).astype(BF16)
    new_head = lax.dynamic_slice_in_dim(new_full, lax.axis_index("fsdp") * shard, shard, 0)
    roll_logits = jnp.dot(rollout, new_full, preferred_element_type=F32)
    action_logp = picked_logp(roll_logits, roll_action)
    return new_head, action_logp, jnp.sum(action_logp.reshape(-1, STEPS), axis=1)


def fits(args, groups, shards):
    hidden, episode, roll, table, head = args[0], args[4], args[5], args[8], args[10]
    if (groups, shards) != (4, 8) or episode.shape[0] != 1:
        return False
    aligned = head.shape[0] % 512 == 0 and head.shape[1] % 128 == 0 and table.shape[0] % 128 == 0
    whole = hidden.shape[1] == shards * head.shape[0] and hidden.shape[0] % 1024 == 0
    return aligned and whole and roll.shape[0] <= 128 and roll.shape[0] % STEPS == 0


def solution(mesh):
    groups, shards = mesh.shape["grp"], mesh.shape["fsdp"]

    def local(*args):
        if not fits(args, groups, shards):
            return local_plain(*args)
        return local_cube(*args)

    both = P(AXES)
    wide = P(AXES, None)
    return jax.shard_map(
        local,
        mesh=mesh,
        in_specs=(wide, both, both, both, wide, wide, both, both, P(), P(), P("fsdp", None)),
        out_specs=(P("fsdp", None), both, both),
        check_vma=False,
    )
```
